32 devices in a mesh: groups: 2 (over y), blk: 4 (over z), head: 4 (over x, core).
Axes of the slice: x: 2, y: 2, z: 4, core: 2. Of those that a mesh axis runs over, the one named last changes fastest.
Arguments:
- queries: bfloat16 [4, 4, 8192], P('groups', 'blk', 'head'), parts along dimension 0, may hold values from -4.5 to 4.5
- stored_cache_keys: bfloat16 [4, 2048, 1024], P('groups', 'blk', 'head'), parts along dimension 0, may hold values from -4.5 to 4.5
- stored_cache_values: bfloat16 [4, 2048, 1024], P('groups', 'blk', 'head'), parts along dimension 0, may hold values from -6 to 6
- out_weight: bfloat16 [8192, 8192], P('head', 'blk'), may hold values from -3 to 3
- lengths: int32 [4], P('groups'), parts along dimension 0, may hold values from 1024 to 2048
Outputs:
- projected: bfloat16 [4, 4, 8192], P('groups', 'head', 'blk'), parts along dimension 0
The draws below stay inside these ranges and needn't reach their ends.
There are 2 independent parts, one for each index of `groups`. The reference program is written for one: setup_inputs(seed, part) draws one part's arguments, and reference() takes and returns one part's arrays. A program takes and returns all parts, laid end to end along the dimension named above; an argument that names none is the same for every part. Nothing has to cross between parts.
All inputs are finite; a program needn't handle non-finite values.
Results may differ from the reference program's by a relative error of at most 0.0056.
Values may be sent and summed in bfloat16 or wider, within the bound.
A program may use at most 64 MiB of HBM per device.

```python
import math
import jax
import jax.numpy as jnp
from jax import lax

REQUEST_COUNT = 2
QUERY_HEAD_COUNT = 64
KEY_VALUE_HEADS = 8
HEAD_DIMENSION = 128
D = 8192
CONTEXT_PER_BLOCK = 512
NEW_TOKENS = 4
CONTEXT_SIZE = 2048
N_BLK = 4


def draw_queries(key, part):
    base_offset = jnp.clip(jax.random.normal(jax.random.fold_in(key, 10), (REQUEST_COUNT, NEW_TOKENS, QUERY_HEAD_COUNT * HEAD_DIMENSION), jnp.float32), -4.5, 4.5)
    return base_offset.astype(jnp.bfloat16)


def draw_stored_cache_keys(key, part):
    base_offset = jnp.clip(jax.random.normal(jax.random.fold_in(key, 11), (REQUEST_COUNT, CONTEXT_SIZE, KEY_VALUE_HEADS * HEAD_DIMENSION), jnp.float32), -4.5, 4.5)
    return base_offset.astype(jnp.bfloat16)


def levels(rng, shape, shards, smallest, high):
    def one(dim, blocks):
        steps = jax.random.uniform(jax.random.fold_in(jax.random.fold_in(rng, 6), dim), (blocks,), jnp.float32, smallest / len(shards), high / len(shards))
        return jnp.repeat(jnp.exp(steps), shape[dim] // blocks).reshape((-1,) + (1,) * (len(shape) - dim - 1))

    gain = one(*shards[0])
    for cut in shards[1:]:
        gain = gain * one(*cut)
    return gain


def gaussian(rng, dims, width, bound, shards=(), kind=jnp.bfloat16):
    gain = levels(rng, dims, shards, -0.22, 0.18) if shards else 1.0
    result = jax.random.normal(rng, dims, jnp.float32) * width * gain
    return jnp.minimum(jnp.maximum(result, -bound), bound).astype(kind)


def setup_inputs(seed: int = 0, part: int = 0) -> dict:
    splits = jax.random.split(jax.random.key(seed), 6)
    own_keys = jax.random.split(jax.random.fold_in(splits[5], part), 6)
    return {
        "queries": draw_queries(jax.random.fold_in(jax.random.fold_in(splits[5], part), 71), part),
        "stored_cache_keys": draw_stored_cache_keys(jax.random.fold_in(jax.random.fold_in(splits[5], part), 71), part),
        "stored_cache_values": gaussian(own_keys[2], (REQUEST_COUNT, CONTEXT_SIZE, KEY_VALUE_HEADS * HEAD_DIMENSION), 1.0, 6.0, ((1, 4), (2, 4))),
        "out_weight": gaussian(splits[3], (QUERY_HEAD_COUNT * HEAD_DIMENSION, D), 0.5, 3.0, ((0, 4), (1, 4))),
        "lengths": jax.random.randint(own_keys[4], (REQUEST_COUNT,), CONTEXT_SIZE // 2, CONTEXT_SIZE + 1).astype(jnp.int32),
    }


masked_fill_value = -1e+30

def reference(queries, stored_cache_keys, stored_cache_values, out_weight, lengths):
    group_width = QUERY_HEAD_COUNT // KEY_VALUE_HEADS
    score_scale = 1.0 / math.sqrt(HEAD_DIMENSION)
    query_float = queries.astype(jnp.float32).reshape(REQUEST_COUNT, NEW_TOKENS, KEY_VALUE_HEADS, group_width, HEAD_DIMENSION)
    query_pos = lengths[:, None] - NEW_TOKENS + jnp.arange(NEW_TOKENS, dtype=jnp.int32)[None, :]

    def advance(carry, block):
        run_max, run_total, run_sum = carry
        first_position = (block * CONTEXT_PER_BLOCK).astype(jnp.int32)
        local_keys = lax.dynamic_slice_in_dim(stored_cache_keys, first_position, CONTEXT_PER_BLOCK, 1).astype(jnp.float32).reshape(REQUEST_COUNT, CONTEXT_PER_BLOCK, KEY_VALUE_HEADS, HEAD_DIMENSION)
        local_values = lax.dynamic_slice_in_dim(stored_cache_values, first_position, CONTEXT_PER_BLOCK, 1).astype(jnp.float32).reshape(REQUEST_COUNT, CONTEXT_PER_BLOCK, KEY_VALUE_HEADS, HEAD_DIMENSION)
        scores = jnp.einsum('rnkgd,rckd->rnkgc', query_float, local_keys) * score_scale
        key_pos = first_position + jnp.arange(CONTEXT_PER_BLOCK, dtype=jnp.int32)
        visible = (key_pos[None, None, :] <= query_pos[:, :, None])[:, :, None, None, :]
        block_max = lax.optimization_barrier(jnp.max(jnp.where(visible, scores, masked_fill_value), axis=-1))
        weights = jnp.where(visible, jnp.exp(scores - block_max[..., None]), 0.0)
        block_total = lax.optimization_barrier(jnp.sum(weights, axis=-1))
        rounded = lax.optimization_barrier(weights.astype(jnp.bfloat16)).astype(jnp.float32)
        block_sum = jnp.einsum('rnkgc,rckd->rnkgd', rounded, local_values)
        new_max = jnp.maximum(run_max, block_max)
        old_factor = jnp.exp(run_max - new_max)
        new_factor = jnp.exp(block_max - new_max)
        run_total = run_total * old_factor + block_total * new_factor
        run_sum = run_sum * old_factor[..., None] + block_sum * new_factor[..., None]
        return ((new_max, run_total, run_sum), None)
    initial_state = (jnp.full((REQUEST_COUNT, NEW_TOKENS, KEY_VALUE_HEADS, group_width), masked_fill_value, jnp.float32), jnp.zeros((REQUEST_COUNT, NEW_TOKENS, KEY_VALUE_HEADS, group_width), jnp.float32), jnp.zeros((REQUEST_COUNT, NEW_TOKENS, KEY_VALUE_HEADS, group_width, HEAD_DIMENSION), jnp.float32))
    final, _ = lax.scan(advance, initial_state, jnp.arange(N_BLK, dtype=jnp.int32))
    run_max, run_total, run_sum = final
    attention = (run_sum / run_total[..., None]).astype(jnp.bfloat16).reshape(REQUEST_COUNT * NEW_TOKENS, QUERY_HEAD_COUNT * HEAD_DIMENSION)
    output = jnp.dot(attention, out_weight, preferred_element_type=jnp.float32)
    return output.astype(jnp.bfloat16).reshape(REQUEST_COUNT, NEW_TOKENS, D)
```

```python
import functools
import math

import jax
import jax.numpy as jnp
from jax import lax
from jax.experimental import pallas as pl
from jax.experimental.pallas import tpu as pltpu
from jax.sharding import PartitionSpec as P

REQUEST_COUNT = 2
QUERY_HEAD_COUNT = 64
KEY_VALUE_HEADS = 8
HEAD_DIMENSION = 128


masked_fill_value = -1e30


MESH = pl.DeviceIdType.MESH
COLUMN_CHUNKS = 4


def fused_kernel(
    dims,
    lengths_ref,
    queries_ref,
    keys_hbm,
    values_hbm,
    weight_hbm,
    out_ref,
    query_slots,
    keys_ref,
    values_ref,
    weight_ref,
    sum_slots,
    stat_slots,
    acc_ref,
    terms_ref,
    term_slots,
    local_sem,
    weight_sem,
    query_send,
    query_recv,
    sum_send,
    sum_recv,
    stat_send,
    stat_recv,
    term_send,
    term_recv,
):
    n_blk, n_head, requests, span, local_heads, group_width = dims
    my_blk = lax.axis_index("blk")
    my_head = lax.axis_index("head")
    rows = n_blk * requests
    stack = group_width * rows
    depth = group_width * HEAD_DIMENSION
    columns = weight_ref.shape[1]
    width = columns // COLUMN_CHUNKS

    key_copy = pltpu.make_async_copy(keys_hbm, keys_ref, local_sem.at[0])
    value_copy = pltpu.make_async_copy(values_hbm, values_ref, local_sem.at[1])
    key_copy.start()
    value_copy.start()
    weight_copies = []
    for kv_head in range(local_heads):
        part = pl.ds(kv_head * depth, depth)
        weight_copies.append(
            pltpu.make_async_copy(
                weight_hbm.at[part], weight_ref.at[part], weight_sem.at[kv_head]
            )
        )
        weight_copies[-1].start()

    barrier = pltpu.get_barrier_semaphore()
    for step in range(1, n_blk):
        peer = lax.rem(my_blk + step, n_blk)
        pl.semaphore_signal(barrier, inc=1, device_id={"blk": peer}, device_id_type=MESH)
    for step in range(1, n_head):
        peer = lax.rem(my_head + step, n_head)
        pl.semaphore_signal(barrier, inc=1, device_id={"head": peer}, device_id_type=MESH)
    pl.semaphore_wait(barrier, n_blk + n_head - 2)

    query_copies = []
    for step in range(1, n_blk):
        copy = pltpu.make_async_remote_copy(
            src_ref=queries_ref,
            dst_ref=query_slots.at[my_blk],
            send_sem=query_send.at[step],
            recv_sem=query_recv.at[step],
            device_id={"blk": lax.rem(my_blk + step, n_blk)},
            device_id_type=MESH,
        )
        copy.start()
        query_copies.append(copy)
    query_slots[my_blk] = queries_ref[...]

    row = lax.broadcasted_iota(jnp.int32, (rows, requests * span), 0)
    column = lax.broadcasted_iota(jnp.int32, (rows, requests * span), 1)
    token, row_request = row // requests, row % requests
    position = my_blk * span + column % span
    visible = jnp.zeros((rows, requests * span), jnp.bool_)
    for request in range(requests):
        here = (column // span == request) & (row_request == request)
        seen = position <= lengths_ref[request] - n_blk + token
        visible = visible | (here & seen)
    visible = visible[None]
    score_scale = 1.0 / math.sqrt(HEAD_DIMENSION)
    lane = lax.broadcasted_iota(jnp.int32, (stack, 128), 1)
    diagonal = lane == lax.broadcasted_iota(jnp.int32, (stack, 128), 0)

    for copy in query_copies:
        copy.wait()
    gathered = jnp.concatenate(
        [query_slots[b].astype(jnp.float32) for b in range(n_blk)], axis=0
    )
    key_copy.wait()
    value_copy.wait()

    partial_copies = []
    for kv_head in range(local_heads):
        entries = pl.ds(kv_head * HEAD_DIMENSION, HEAD_DIMENSION)
        block_query = jnp.concatenate(
            [
                gathered[:, h * HEAD_DIMENSION : (h + 1) * HEAD_DIMENSION]
                for h in range(kv_head * group_width, (kv_head + 1) * group_width)
            ],
            axis=0,
        ).astype(jnp.bfloat16)
        scores = lax.dot_general(
            block_query,
            keys_ref[:, entries],
            (((1,), (1,)), ((), ())),
            preferred_element_type=jnp.float32,
        )
        scores = (scores * score_scale).reshape(group_width, rows, requests * span)
        block_max = jnp.max(
            jnp.where(visible, scores, masked_fill_value), axis=-1, keepdims=True
        )
        weights = jnp.where(visible, jnp.exp(scores - block_max), 0.0)
        total = jnp.sum(weights, axis=-1, keepdims=True)
        weighted = jnp.dot(
            weights.reshape(stack, requests * span).astype(jnp.bfloat16),
            values_ref[:, entries],
            preferred_element_type=jnp.float32,
        )
        sum_slots[kv_head, my_blk] = weighted.astype(sum_slots.dtype)
        stats = [
            jnp.sum(jnp.where(diagonal, x.reshape(stack, 1), 0.0), axis=0, keepdims=True)
            for x in (block_max, total)
        ]
        stat_slots[kv_head, my_blk] = jnp.concatenate(
            stats + [jnp.zeros((6, 128), jnp.float32)], axis=0
        )
        copies = []
        for step in range(1, n_blk):
            peer = lax.rem(my_blk + step, n_blk)
            for slots, send, recv in (
                (stat_slots, stat_send, stat_recv),
                (sum_slots, sum_send, sum_recv),
            ):
                copy = pltpu.make_async_remote_copy(
                    src_ref=slots.at[kv_head, my_blk],
                    dst_ref=slots.at[kv_head, my_blk],
                    send_sem=send.at[kv_head, step],
                    recv_sem=recv.at[kv_head, step],
                    device_id={"blk": peer},
                    device_id_type=MESH,
                )
                copy.start()
                copies.append(copy)
        partial_copies.append(copies)

    term_copies = []
    for kv_head in range(local_heads):
        for copy in partial_copies[kv_head]:
            copy.wait()
        maxima = [stat_slots[kv_head, b, 0:1, :] for b in range(n_blk)]
        totals = [stat_slots[kv_head, b, 1:2, :] for b in range(n_blk)]
        top = functools.reduce(jnp.maximum, maxima)
        factors = [jnp.exp(x - top) for x in maxima]
        overall = sum(f * x for f, x in zip(factors, totals))
        overall = jnp.where(lane[0:1] < stack, overall, 1.0)
        merged = jnp.zeros((stack, HEAD_DIMENSION), jnp.float32)
        for b in range(n_blk):
            share = jnp.sum(
                jnp.where(diagonal, factors[b] / overall, 0.0), axis=1, keepdims=True
            )
            merged = merged + sum_slots[kv_head, b].astype(jnp.float32) * share
        attention = jnp.concatenate(
            [merged[g * rows : (g + 1) * rows] for g in range(group_width)], axis=1
        ).astype(jnp.bfloat16)
        weight_copies[kv_head].wait()
        part = pl.ds(kv_head * depth, depth)
        for chunk in range(COLUMN_CHUNKS):
            where = pl.ds(chunk * width, width)
            term = jnp.dot(
                attention, weight_ref[part, where], preferred_element_type=jnp.float32
            )
            if kv_head > 0:
                term = term + acc_ref[:, where]
            if kv_head < local_heads - 1:
                acc_ref[:, where] = term
                continue
            for h in range(n_head):
                terms_ref[chunk, h] = term[h * requests : (h + 1) * requests]
            for step in range(1, n_head):
                peer = lax.rem(my_head + step, n_head)
                copy = pltpu.make_async_remote_copy(
                    src_ref=terms_ref.at[chunk, peer],
                    dst_ref=term_slots.at[chunk, step],
                    send_sem=term_send.at[chunk, step],
                    recv_sem=term_recv.at[chunk, step],
                    device_id={"head": peer},
                    device_id_type=MESH,
                )
                copy.start()
                term_copies.append(copy)

    for chunk in range(COLUMN_CHUNKS):
        result = terms_ref[chunk, my_head]
        for step in range(1, n_head):
            term_copies[chunk * (n_head - 1) + step - 1].wait()
            result = result + term_slots[chunk, step]
        out_ref[:, pl.ds(chunk * width, width)] = result.astype(out_ref.dtype)


def fused(queries, stored_cache_keys, stored_cache_values, out_weight, lengths):
    n_blk, n_head = lax.axis_size("blk"), lax.axis_size("head")
    requests, span, kv_width = stored_cache_keys.shape
    group_width = QUERY_HEAD_COUNT // KEY_VALUE_HEADS
    local_heads = kv_width // HEAD_DIMENSION
    inputs, columns = out_weight.shape
    rows = requests * n_blk
    stack = group_width * rows
    width = columns // COLUMN_CHUNKS
    dims = (n_blk, n_head, requests, span, local_heads, group_width)
    vmem = pl.BlockSpec(memory_space=pltpu.VMEM)
    hbm = pl.BlockSpec(memory_space=pl.ANY)
    out = pl.pallas_call(
        functools.partial(fused_kernel, dims),
        out_shape=jax.ShapeDtypeStruct((requests, columns), jnp.bfloat16),
        in_specs=[pl.BlockSpec(memory_space=pltpu.SMEM), vmem, hbm, hbm, hbm],
        out_specs=vmem,
        scratch_shapes=[
            pltpu.VMEM((n_blk, requests, inputs), jnp.bfloat16),
            pltpu.VMEM((requests * span, kv_width), jnp.bfloat16),
            pltpu.VMEM((requests * span, kv_width), jnp.bfloat16),
            pltpu.VMEM((inputs, columns), jnp.bfloat16),
            pltpu.VMEM((local_heads, n_blk, stack, HEAD_DIMENSION), jnp.bfloat16),
            pltpu.VMEM((local_heads, n_blk, 8, 128), jnp.float32),
            pltpu.VMEM((rows, columns), jnp.float32),
            pltpu.VMEM((COLUMN_CHUNKS, n_head, requests, width), jnp.float32),
            pltpu.VMEM((COLUMN_CHUNKS, n_head, requests, width), jnp.float32),
            pltpu.SemaphoreType.DMA((2,)),
            pltpu.SemaphoreType.DMA((local_heads,)),
            pltpu.SemaphoreType.DMA((n_blk,)),
            pltpu.SemaphoreType.DMA((n_blk,)),
            pltpu.SemaphoreType.DMA((local_heads, n_blk)),
            pltpu.SemaphoreType.DMA((local_heads, n_blk)),
            pltpu.SemaphoreType.DMA((local_heads, n_blk)),
            pltpu.SemaphoreType.DMA((local_heads, n_blk)),
            pltpu.SemaphoreType.DMA((COLUMN_CHUNKS, n_head)),
            pltpu.SemaphoreType.DMA((COLUMN_CHUNKS, n_head)),
        ],
        compiler_params=pltpu.CompilerParams(collective_id=0, has_side_effects=True),
    )(
        lengths,
        queries.reshape(requests, inputs),
        stored_cache_keys.reshape(requests * span, kv_width),
        stored_cache_values.reshape(requests * span, kv_width),
        out_weight,
    )
    return out.reshape(requests, 1, columns)


def layer(queries, stored_cache_keys, *others):
    tokens = queries.shape[1] * lax.axis_size("blk")
    fits = (
        queries.shape[1] == 1
        and tokens == lax.axis_size("head")
        and tokens * queries.shape[0] == 8
    )
    return (fused if fits else body)(queries, stored_cache_keys, *others)


def body(queries, stored_cache_keys, stored_cache_values, out_weight, lengths):
    group_width = QUERY_HEAD_COUNT // KEY_VALUE_HEADS
    local_heads = stored_cache_keys.shape[2] // HEAD_DIMENSION
    query_heads = local_heads * group_width
    span = stored_cache_keys.shape[1]
    new_count = queries.shape[1] * lax.axis_size("blk")
    key_pos = lax.axis_index("blk") * span + jnp.arange(span, dtype=jnp.int32)
    score_scale = 1.0 / math.sqrt(HEAD_DIMENSION)
    piece = lax.all_gather(queries, "blk", axis=1, tiled=True)
    rows_count = piece.shape[1]
    query_pos = lengths[:, None] - new_count + jnp.arange(rows_count, dtype=jnp.int32)[None, :]
    sums_list = []
    maxima_list = []
    totals_list = []
    for request in range(REQUEST_COUNT):
        visible = (key_pos[None, :] <= query_pos[request][:, None])[:, None, :]
        parts_sum, parts_max, parts_total = ([], [], [])
        for kv_head in range(local_heads):
            block_query = piece[
                request,
                :,
                kv_head
                * group_width
                * HEAD_DIMENSION : (kv_head + 1)
                * group_width
                * HEAD_DIMENSION,
            ].reshape(rows_count, group_width, HEAD_DIMENSION)
            local_keys = stored_cache_keys[
                request, :, kv_head * HEAD_DIMENSION : (kv_head + 1) * HEAD_DIMENSION
            ]
            local_values = stored_cache_values[
                request, :, kv_head * HEAD_DIMENSION : (kv_head + 1) * HEAD_DIMENSION
            ]
            scores = (
                jnp.einsum(
                    "ngd,cd->ngc", block_query, local_keys, preferred_element_type=jnp.float32
                )
                * score_scale
            )
            block_max = jnp.max(jnp.where(visible, scores, masked_fill_value), axis=-1)
            weights = jnp.where(visible, jnp.exp(scores - block_max[..., None]), 0.0)
            parts_total.append(jnp.sum(weights, axis=-1))
            parts_max.append(block_max)
            weighted = jnp.einsum(
                "ngc,cd->ngd",
                weights.astype(jnp.bfloat16),
                local_values,
                preferred_element_type=jnp.float32,
            )
            parts_sum.append(weighted.reshape(rows_count, group_width * HEAD_DIMENSION))
        sums_list.append(jnp.concatenate(parts_sum, axis=1))
        maxima_list.append(jnp.concatenate(parts_max, axis=1))
        totals_list.append(jnp.concatenate(parts_total, axis=1))
    new_sums = jnp.stack(sums_list, axis=0)
    new_maxima = jnp.stack(maxima_list, axis=0)
    new_totals = jnp.stack(totals_list, axis=0)
    received = (
        lax.all_to_all(new_sums[None], "blk", split_axis=2, concat_axis=0, tiled=True),
        lax.all_to_all(new_maxima[None], "blk", split_axis=2, concat_axis=0, tiled=True),
        lax.all_to_all(new_totals[None], "blk", split_axis=2, concat_axis=0, tiled=True),
    )
    part_sums, part_max, part_totals = received
    blocks = part_sums.shape[0]
    own_rows = part_sums.shape[2]
    top = jnp.max(part_max, axis=0)
    factor = jnp.exp(part_max - top[None])
    overall = jnp.sum(factor * part_totals, axis=0)
    shaped = part_sums.reshape(blocks, REQUEST_COUNT, own_rows, query_heads, HEAD_DIMENSION)
    merged = jnp.sum(shaped * factor[..., None], axis=0) / overall[..., None]
    own_attention = merged.astype(jnp.bfloat16).reshape(
        REQUEST_COUNT, own_rows, query_heads * HEAD_DIMENSION
    )
    terms = jnp.einsum(
        "rnc,cd->rnd",
        lax.all_gather(own_attention, "blk", axis=1, tiled=True),
        out_weight,
        preferred_element_type=jnp.float32,
    )
    return lax.psum_scatter(terms, "head", scatter_dimension=1, tiled=True).astype(jnp.bfloat16)


def solution(mesh):
    placed = (
        P("groups", "blk", "head"),
        P("groups", "blk", "head"),
        P("groups", "blk", "head"),
        P("head", "blk"),
        P("groups"),
    )
    return jax.shard_map(
        layer, mesh=mesh, in_specs=placed, out_specs=P("groups", "head", "blk"), check_vma=False
    )
```

```python
import functools
import math

import jax
import jax.numpy as jnp
from jax import lax
from jax.experimental import pallas as pl
from jax.experimental.pallas import tpu as pltpu
from jax.sharding import PartitionSpec as P

REQUEST_COUNT = 2
QUERY_HEAD_COUNT = 64
KEY_VALUE_HEADS = 8
HEAD_DIMENSION = 128


masked_fill_value = -1e30


MESH = pl.DeviceIdType.MESH
COLUMN_CHUNKS = 1
LANES = 128


def fused_kernel(
    dims,
    lengths_hbm,
    queries_hbm,
    keys_hbm,
    values_hbm,
    weight_hbm,
    out_ref,
    lengths_ref,
    query_slots,
    keys_ref,
    values_ref,
    weight_ref,
    sum_slots,
    stat_slots,
    acc_ref,
    terms_ref,
    term_slots,
    local_sem,
    weight_sem,
    query_send,
    query_recv,
    sum_send,
    sum_recv,
    stat_send,
    stat_recv,
    term_send,
    term_recv,
):
    n_blk, n_head, requests, span, local_heads, group_width = dims
    my_blk = lax.axis_index("blk")
    my_head = lax.axis_index("head")
    rows = n_blk * requests
    stack = group_width * rows
    depth = group_width * HEAD_DIMENSION
    columns = weight_ref.shape[1]
    width = columns // COLUMN_CHUNKS

    barrier = pltpu.get_barrier_semaphore()
    for step in range(1, n_blk):
        peer = lax.rem(my_blk + step, n_blk)
        pl.semaphore_signal(barrier, inc=1, device_id={"blk": peer}, device_id_type=MESH)
    for step in range(1, n_head):
        peer = lax.rem(my_head + step, n_head)
        pl.semaphore_signal(barrier, inc=1, device_id={"head": peer}, device_id_type=MESH)
    query_copy = pltpu.make_async_copy(
        queries_hbm, query_slots.at[my_blk], local_sem.at[2]
    )
    query_copy.start()
    length_copy = pltpu.make_async_copy(lengths_hbm, lengths_ref, local_sem.at[3])
    length_copy.start()
    key_copy = pltpu.make_async_copy(keys_hbm, keys_ref, local_sem.at[0])
    value_copy = pltpu.make_async_copy(values_hbm, values_ref, local_sem.at[1])
    key_copy.start()
    value_copy.start()
    weight_copies = []
    for kv_head in range(local_heads):
        part = pl.ds(kv_head * depth, depth)
        weight_copies.append(
            pltpu.make_async_copy(
                weight_hbm.at[part], weight_ref.at[part], weight_sem.at[kv_head]
            )
        )
        weight_copies[-1].start()

    query_copy.wait()
    pl.semaphore_wait(barrier, n_blk + n_head - 2)

    query_copies = []
    for step in range(1, n_blk):
        copy = pltpu.make_async_remote_copy(
            src_ref=query_slots.at[my_blk],
            dst_ref=query_slots.at[my_blk],
            send_sem=query_send.at[step],
            recv_sem=query_recv.at[step],
            device_id={"blk": lax.rem(my_blk + step, n_blk)},
            device_id_type=MESH,
        )
        copy.start()
        query_copies.append(copy)
    length_copy.wait()

    row = lax.broadcasted_iota(jnp.int32, (rows, requests * span), 0)
    column = lax.broadcasted_iota(jnp.int32, (rows, requests * span), 1)
    token, row_request = row // requests, row % requests
    position = my_blk * span + column % span
    visible = jnp.zeros((rows, requests * span), jnp.bool_)
    for request in range(requests):
        here = (column // span == request) & (row_request == request)
        seen = position <= lengths_ref[request] - n_blk + token
        visible = visible | (here & seen)
    visible = visible[None]
    score_scale = 1.0 / math.sqrt(HEAD_DIMENSION)
    lane = lax.broadcasted_iota(jnp.int32, (stack, LANES), 1)
    own_lane = lax.broadcasted_iota(jnp.int32, (stack, LANES), 0)
    max_place, total_place = lane == own_lane, lane == own_lane + LANES // 2

    for copy in query_copies:
        copy.wait()
    gathered = jnp.concatenate(
        [query_slots[b].astype(jnp.float32) for b in range(n_blk)], axis=0
    )
    key_copy.wait()
    value_copy.wait()

    partial_copies = []
    for kv_head in range(local_heads):
        entries = pl.ds(kv_head * HEAD_DIMENSION, HEAD_DIMENSION)
        block_query = jnp.concatenate(
            [
                gathered[:, h * HEAD_DIMENSION : (h + 1) * HEAD_DIMENSION]
                for h in range(kv_head * group_width, (kv_head + 1) * group_width)
            ],
            axis=0,
        ).astype(jnp.bfloat16)
        scores = lax.dot_general(
            block_query,
            keys_ref[:, entries],
            (((1,), (1,)), ((), ())),
            preferred_element_type=jnp.float32,
        )
        scores = (scores * score_scale).reshape(group_width, rows, requests * span)
        block_max = jnp.max(
            jnp.where(visible, scores, masked_fill_value), axis=-1, keepdims=True
        )
        weights = jnp.where(visible, jnp.exp(scores - block_max), 0.0)
        total = jnp.sum(weights, axis=-1, keepdims=True)
        weighted = jnp.dot(
            weights.reshape(stack, requests * span).astype(jnp.bfloat16),
            values_ref[:, entries],
            preferred_element_type=jnp.float32,
        )
        sum_slots[kv_head, my_blk] = weighted.astype(sum_slots.dtype)
        stats = jnp.where(
            max_place,
            block_max.reshape(stack, 1),
            jnp.where(total_place, total.reshape(stack, 1), 0.0),
        )
        stat_slots[kv_head, my_blk] = jnp.sum(stats, axis=0, keepdims=True)
        copies = []
        for step in range(1, n_blk):
            peer = lax.rem(my_blk + step, n_blk)
            for slots, send, recv in (
                (stat_slots, stat_send, stat_recv),
                (sum_slots, sum_send, sum_recv),
            ):
                copy = pltpu.make_async_remote_copy(
                    src_ref=slots.at[kv_head, my_blk],
                    dst_ref=slots.at[kv_head, my_blk],
                    send_sem=send.at[kv_head, step],
                    recv_sem=recv.at[kv_head, step],
                    device_id={"blk": peer},
                    device_id_type=MESH,
                )
                copy.start()
                copies.append(copy)
        partial_copies.append(copies)

    term_copies = []
    for kv_head in range(local_heads):
        for copy in partial_copies[kv_head]:
            copy.wait()
        maxima = [stat_slots[kv_head, b] for b in range(n_blk)]
        totals = [pltpu.roll(x, LANES // 2, 1) for x in maxima]
        top = functools.reduce(jnp.maximum, maxima)
        factors = [jnp.exp(x - top) for x in maxima]
        overall = sum(f * x for f, x in zip(factors, totals))
        overall = jnp.where(lane[0:1] < stack, overall, 1.0)
        merged = jnp.zeros((stack, HEAD_DIMENSION), jnp.float32)
        for b in range(n_blk):
            share = jnp.sum(
                jnp.where(max_place, factors[b] / overall, 0.0), axis=1, keepdims=True
            )
            merged = merged + sum_slots[kv_head, b].astype(jnp.float32) * share
        attention = jnp.concatenate(
            [merged[g * rows : (g + 1) * rows] for g in range(group_width)], axis=1
        ).astype(jnp.bfloat16)
        weight_copies[kv_head].wait()
        part = pl.ds(kv_head * depth, depth)
        for chunk in range(COLUMN_CHUNKS):
            where = pl.ds(chunk * width, width)
            term = jnp.dot(
                attention, weight_ref[part, where], preferred_element_type=jnp.float32
            )
            if kv_head > 0:
                term = term + acc_ref[:, where]
            if kv_head < local_heads - 1:
                acc_ref[:, where] = term
                continue
            for h in range(n_head):
                terms_ref[chunk, h] = term[h * requests : (h + 1) * requests]
            for step in range(1, n_head):
                peer = lax.rem(my_head + step, n_head)
                copy = pltpu.make_async_remote_copy(
                    src_ref=terms_ref.at[chunk, peer],
                    dst_ref=term_slots.at[chunk, step],
                    send_sem=term_send.at[chunk, step],
                    recv_sem=term_recv.at[chunk, step],
                    device_id={"head": peer},
                    device_id_type=MESH,
                )
                copy.start()
                term_copies.append(copy)

    for chunk in range(COLUMN_CHUNKS):
        result = terms_ref[chunk, my_head]
        for step in range(1, n_head):
            term_copies[chunk * (n_head - 1) + step - 1].wait()
            result = result + term_slots[chunk, step]
        out_ref[:, pl.ds(chunk * width, width)] = result.astype(out_ref.dtype)


def fused(queries, stored_cache_keys, stored_cache_values, out_weight, lengths):
    n_blk, n_head = lax.axis_size("blk"), lax.axis_size("head")
    requests, span, kv_width = stored_cache_keys.shape
    group_width = QUERY_HEAD_COUNT // KEY_VALUE_HEADS
    local_heads = kv_width // HEAD_DIMENSION
    inputs, columns = out_weight.shape
    rows = requests * n_blk
    stack = group_width * rows
    width = columns // COLUMN_CHUNKS
    dims = (n_blk, n_head, requests, span, local_heads, group_width)
    vmem = pl.BlockSpec(memory_space=pltpu.VMEM)
    hbm = pl.BlockSpec(memory_space=pl.ANY)
    out = pl.pallas_call(
        functools.partial(fused_kernel, dims),
        out_shape=jax.ShapeDtypeStruct((requests, columns), jnp.bfloat16),
        in_specs=[hbm] * 5,
        out_specs=vmem,
        scratch_shapes=[
            pltpu.SMEM((requests,), jnp.int32),
            pltpu.VMEM((n_blk, requests, inputs), jnp.bfloat16),
            pltpu.VMEM((requests * span, kv_width), jnp.bfloat16),
            pltpu.VMEM((requests * span, kv_width), jnp.bfloat16),
            pltpu.VMEM((inputs, columns), jnp.bfloat16),
            pltpu.VMEM((local_heads, n_blk, stack, HEAD_DIMENSION), jnp.bfloat16),
            pltpu.VMEM((local_heads, n_blk, 1, LANES), jnp.float32),
            pltpu.VMEM((rows, columns), jnp.float32),
            pltpu.VMEM((COLUMN_CHUNKS, n_head, requests, width), jnp.float32),
            pltpu.VMEM((COLUMN_CHUNKS, n_head, requests, width), jnp.float32),
            pltpu.SemaphoreType.DMA((4,)),
            pltpu.SemaphoreType.DMA((local_heads,)),
            pltpu.SemaphoreType.DMA((n_blk,)),
            pltpu.SemaphoreType.DMA((n_blk,)),
            pltpu.SemaphoreType.DMA((local_heads, n_blk)),
            pltpu.SemaphoreType.DMA((local_heads, n_blk)),
            pltpu.SemaphoreType.DMA((local_heads, n_blk)),
            pltpu.SemaphoreType.DMA((local_heads, n_blk)),
            pltpu.SemaphoreType.DMA((COLUMN_CHUNKS, n_head)),
            pltpu.SemaphoreType.DMA((COLUMN_CHUNKS, n_head)),
        ],
        compiler_params=pltpu.CompilerParams(collective_id=0, has_side_effects=True),
    )(
        lengths,
        queries.reshape(requests, inputs),
        stored_cache_keys.reshape(requests * span, kv_width),
        stored_cache_values.reshape(requests * span, kv_width),
        out_weight,
    )
    return out.reshape(requests, 1, columns)


def layer(queries, stored_cache_keys, *others):
    tokens = queries.shape[1] * lax.axis_size("blk")
    fits = (
        queries.shape[1] == 1
        and tokens == lax.axis_size("head")
        and tokens * queries.shape[0] == 8
        and QUERY_HEAD_COUNT // KEY_VALUE_HEADS * 8 == LANES // 2
    )
    return (fused if fits else body)(queries, stored_cache_keys, *others)


def body(queries, stored_cache_keys, stored_cache_values, out_weight, lengths):
    group_width = QUERY_HEAD_COUNT // KEY_VALUE_HEADS
    local_heads = stored_cache_keys.shape[2] // HEAD_DIMENSION
    query_heads = local_heads * group_width
    span = stored_cache_keys.shape[1]
    new_count = queries.shape[1] * lax.axis_size("blk")
    key_pos = lax.axis_index("blk") * span + jnp.arange(span, dtype=jnp.int32)
    score_scale = 1.0 / math.sqrt(HEAD_DIMENSION)
    piece = lax.all_gather(queries, "blk", axis=1, tiled=True)
    rows_count = piece.shape[1]
    query_pos = lengths[:, None] - new_count + jnp.arange(rows_count, dtype=jnp.int32)[None, :]
    sums_list = []
    maxima_list = []
    totals_list = []
    for request in range(REQUEST_COUNT):
        visible = (key_pos[None, :] <= query_pos[request][:, None])[:, None, :]
        parts_sum, parts_max, parts_total = ([], [], [])
        for kv_head in range(local_heads):
            block_query = piece[
                request,
                :,
                kv_head
                * group_width
                * HEAD_DIMENSION : (kv_head + 1)
                * group_width
                * HEAD_DIMENSION,
            ].reshape(rows_count, group_width, HEAD_DIMENSION)
            local_keys = stored_cache_keys[
                request, :, kv_head * HEAD_DIMENSION : (kv_head + 1) * HEAD_DIMENSION
            ]
            local_values = stored_cache_values[
                request, :, kv_head * HEAD_DIMENSION : (kv_head + 1) * HEAD_DIMENSION
            ]
            scores = (
                jnp.einsum(
                    "ngd,cd->ngc", block_query, local_keys, preferred_element_type=jnp.float32
                )
                * score_scale
            )
            block_max = jnp.max(jnp.where(visible, scores, masked_fill_value), axis=-1)
            weights = jnp.where(visible, jnp.exp(scores - block_max[..., None]), 0.0)
            parts_total.append(jnp.sum(weights, axis=-1))
            parts_max.append(block_max)
            weighted = jnp.einsum(
                "ngc,cd->ngd",
                weights.astype(jnp.bfloat16),
                local_values,
                preferred_element_type=jnp.float32,
            )
            parts_sum.append(weighted.reshape(rows_count, group_width * HEAD_DIMENSION))
        sums_list.append(jnp.concatenate(parts_sum, axis=1))
        maxima_list.append(jnp.concatenate(parts_max, axis=1))
        totals_list.append(jnp.concatenate(parts_total, axis=1))
    new_sums = jnp.stack(sums_list, axis=0)
    new_maxima = jnp.stack(maxima_list, axis=0)
    new_totals = jnp.stack(totals_list, axis=0)
    received = (
        lax.all_to_all(new_sums[None], "blk", split_axis=2, concat_axis=0, tiled=True),
        lax.all_to_all(new_maxima[None], "blk", split_axis=2, concat_axis=0, tiled=True),
        lax.all_to_all(new_totals[None], "blk", split_axis=2, concat_axis=0, tiled=True),
    )
    part_sums, part_max, part_totals = received
    blocks = part_sums.shape[0]
    own_rows = part_sums.shape[2]
    top = jnp.max(part_max, axis=0)
    factor = jnp.exp(part_max - top[None])
    overall = jnp.sum(factor * part_totals, axis=0)
    shaped = part_sums.reshape(blocks, REQUEST_COUNT, own_rows, query_heads, HEAD_DIMENSION)
    merged = jnp.sum(shaped * factor[..., None], axis=0) / overall[..., None]
    own_attention = merged.astype(jnp.bfloat16).reshape(
        REQUEST_COUNT, own_rows, query_heads * HEAD_DIMENSION
    )
    terms = jnp.einsum(
        "rnc,cd->rnd",
        lax.all_gather(own_attention, "blk", axis=1, tiled=True),
        out_weight,
        preferred_element_type=jnp.float32,
    )
    return lax.psum_scatter(terms, "head", scatter_dimension=1, tiled=True).astype(jnp.bfloat16)


def solution(mesh):
    placed = (
        P("groups", "blk", "head"),
        P("groups", "blk", "head"),
        P("groups", "blk", "head"),
        P("head", "blk"),
        P("groups"),
    )
    return jax.shard_map(
        layer, mesh=mesh, in_specs=placed, out_specs=P("groups", "head", "blk"), check_vma=False
    )
```

```python
import functools
import math

import jax
import jax.numpy as jnp
from jax import lax
from jax.experimental import pallas as pl
from jax.experimental.pallas import tpu as pltpu
from jax.sharding import PartitionSpec as P

REQUEST_COUNT = 2
QUERY_HEAD_COUNT = 64
KEY_VALUE_HEADS = 8
HEAD_DIMENSION = 128


masked_fill_value = -1e30


MESH = pl.DeviceIdType.MESH
COLUMN_CHUNKS = 1
LANES = 128


def fused_kernel(
    dims,
    lengths_hbm,
    queries_hbm,
    keys_hbm,
    values_hbm,
    weight_hbm,
    parts_hbm,
    lengths_ref,
    query_slots,
    keys_ref,
    values_ref,
    weight_ref,
    sum_slots,
    stat_slots,
    acc_ref,
    terms_ref,
    local_sem,
    weight_sem,
    query_send,
    query_recv,
    sum_send,
    sum_recv,
    stat_send,
    stat_recv,
    term_send,
    term_recv,
):
    n_blk, n_head, requests, span, local_heads, group_width = dims
    my_blk = lax.axis_index("blk")
    my_head = lax.axis_index("head")
    rows = n_blk * requests
    stack = group_width * rows
    depth = group_width * HEAD_DIMENSION
    columns = weight_ref.shape[1]
    width = columns // COLUMN_CHUNKS

    barrier = pltpu.get_barrier_semaphore()
    for step in range(1, n_blk):
        peer = lax.rem(my_blk + step, n_blk)
        pl.semaphore_signal(barrier, inc=1, device_id={"blk": peer}, device_id_type=MESH)
    for step in range(1, n_head):
        peer = lax.rem(my_head + step, n_head)
        pl.semaphore_signal(barrier, inc=1, device_id={"head": peer}, device_id_type=MESH)
    query_copy = pltpu.make_async_copy(
        queries_hbm, query_slots.at[my_blk], local_sem.at[2]
    )
    query_copy.start()
    length_copy = pltpu.make_async_copy(lengths_hbm, lengths_ref, local_sem.at[3])
    length_copy.start()
    key_copy = pltpu.make_async_copy(keys_hbm, keys_ref, local_sem.at[0])
    value_copy = pltpu.make_async_copy(values_hbm, values_ref, local_sem.at[1])
    key_copy.start()
    value_copy.start()
    weight_copies = []
    for kv_head in range(local_heads):
        part = pl.ds(kv_head * depth, depth)
        weight_copies.append(
            pltpu.make_async_copy(
                weight_hbm.at[part], weight_ref.at[part], weight_sem.at[kv_head]
            )
        )
        weight_copies[-1].start()

    query_copy.wait()
    pl.semaphore_wait(barrier, n_blk + n_head - 2)

    peers = []
    for k in range(n_blk - 1):
        down = n_blk - 1 - k
        down = jnp.where(down <= my_blk, down - 1, down)
        up = jnp.where(k >= my_blk, k + 1, k)
        peers.append(jnp.where(my_blk < n_blk // 2, down, up))

    query_copies = []
    for peer in peers:
        copy = pltpu.make_async_remote_copy(
            src_ref=query_slots.at[my_blk],
            dst_ref=query_slots.at[my_blk],
            send_sem=query_send.at[peer],
            recv_sem=query_recv.at[my_blk],
            device_id={"blk": peer},
            device_id_type=MESH,
        )
        copy.start()
        query_copies.append(copy)
    length_copy.wait()

    row = lax.broadcasted_iota(jnp.int32, (rows, requests * span), 0)
    column = lax.broadcasted_iota(jnp.int32, (rows, requests * span), 1)
    token, row_request = row // requests, row % requests
    position = my_blk * span + column % span
    visible = jnp.zeros((rows, requests * span), jnp.bool_)
    for request in range(requests):
        here = (column // span == request) & (row_request == request)
        seen = position <= lengths_ref[request] - n_blk + token
        visible = visible | (here & seen)
    visible = visible[None]
    score_scale = 1.0 / math.sqrt(HEAD_DIMENSION)
    lane = lax.broadcasted_iota(jnp.int32, (stack, LANES), 1)
    own_lane = lax.broadcasted_iota(jnp.int32, (stack, LANES), 0)
    max_place, total_place = lane == own_lane, lane == own_lane + LANES // 2

    for peer, copy in zip(peers, query_copies):
        pltpu.make_async_copy(
            query_slots.at[peer], query_slots.at[peer], query_recv.at[peer]
        ).wait()
    gathered = jnp.concatenate(
        [query_slots[b].astype(jnp.float32) for b in range(n_blk)], axis=0
    )
    key_copy.wait()
    value_copy.wait()

    partial_copies = []
    for kv_head in range(local_heads):
        entries = pl.ds(kv_head * HEAD_DIMENSION, HEAD_DIMENSION)
        block_query = jnp.concatenate(
            [
                gathered[:, h * HEAD_DIMENSION : (h + 1) * HEAD_DIMENSION]
                for h in range(kv_head * group_width, (kv_head + 1) * group_width)
            ],
            axis=0,
        ).astype(jnp.bfloat16)
        scores = lax.dot_general(
            block_query,
            keys_ref[:, entries],
            (((1,), (1,)), ((), ())),
            preferred_element_type=jnp.float32,
        )
        scores = (scores * score_scale).reshape(group_width, rows, requests * span)
        block_max = jnp.max(
            jnp.where(visible, scores, masked_fill_value), axis=-1, keepdims=True
        )
        weights = jnp.where(visible, jnp.exp(scores - block_max), 0.0)
        total = jnp.sum(weights, axis=-1, keepdims=True)
        weighted = jnp.dot(
            weights.reshape(stack, requests * span).astype(jnp.bfloat16),
            values_ref[:, entries],
            preferred_element_type=jnp.float32,
        )
        sum_slots[kv_head, my_blk] = weighted.astype(sum_slots.dtype)
        stats = jnp.where(
            max_place,
            block_max.reshape(stack, 1),
            jnp.where(total_place, total.reshape(stack, 1), 0.0),
        )
        stat_slots[kv_head, my_blk] = jnp.sum(stats, axis=0, keepdims=True)
        copies = []
        for peer in peers:
            for slots, send, recv in (
                (stat_slots, stat_send, stat_recv),
                (sum_slots, sum_send, sum_recv),
            ):
                copy = pltpu.make_async_remote_copy(
                    src_ref=slots.at[kv_head, my_blk],
                    dst_ref=slots.at[kv_head, my_blk],
                    send_sem=send.at[kv_head, peer],
                    recv_sem=recv.at[kv_head, my_blk],
                    device_id={"blk": peer},
                    device_id_type=MESH,
                )
                copy.start()
                copies.append(copy)
        partial_copies.append(copies)

    term_copies = []
    for kv_head in range(local_heads):
        for peer in peers:
            for slots, recv in ((stat_slots, stat_recv), (sum_slots, sum_recv)):
                here = slots.at[kv_head, peer]
                pltpu.make_async_copy(here, here, recv.at[kv_head, peer]).wait()
        maxima = [stat_slots[kv_head, b] for b in range(n_blk)]
        totals = [pltpu.roll(x, LANES // 2, 1) for x in maxima]
        top = functools.reduce(jnp.maximum, maxima)
        factors = [jnp.exp(x - top) for x in maxima]
        overall = sum(f * x for f, x in zip(factors, totals))
        overall = jnp.where(lane[0:1] < stack, overall, 1.0)
        merged = jnp.zeros((stack, HEAD_DIMENSION), jnp.float32)
        for b in range(n_blk):
            share = jnp.sum(
                jnp.where(max_place, factors[b] / overall, 0.0), axis=1, keepdims=True
            )
            merged = merged + sum_slots[kv_head, b].astype(jnp.float32) * share
        attention = jnp.concatenate(
            [merged[g * rows : (g + 1) * rows] for g in range(group_width)], axis=1
        ).astype(jnp.bfloat16)
        weight_copies[kv_head].wait()
        part = pl.ds(kv_head * depth, depth)
        for chunk in range(COLUMN_CHUNKS):
            where = pl.ds(chunk * width, width)
            term = jnp.dot(
                attention, weight_ref[part, where], preferred_element_type=jnp.float32
            )
            if kv_head > 0:
                term = term + acc_ref[:, where]
            if kv_head < local_heads - 1:
                acc_ref[:, where] = term
                continue
            for h in range(n_head):
                terms_ref[chunk, h] = term[h * requests : (h + 1) * requests]
            own_copy = pltpu.make_async_copy(
                terms_ref.at[chunk, my_head],
                parts_hbm.at[chunk, my_head],
                term_send.at[chunk, 0],
            )
            own_copy.start()
            term_copies.append(own_copy)
            for step in range(1, n_head):
                peer = lax.rem(my_head + step, n_head)
                copy = pltpu.make_async_remote_copy(
                    src_ref=terms_ref.at[chunk, peer],
                    dst_ref=parts_hbm.at[chunk, my_head],
                    send_sem=term_send.at[chunk, step],
                    recv_sem=term_recv.at[chunk, step],
                    device_id={"head": peer},
                    device_id_type=MESH,
                )
                copy.start()
                term_copies.append(copy)

    for copy in term_copies:
        copy.wait()
    for copies in [query_copies] + partial_copies:
        for copy in copies:
            copy.wait_send()


def fused(queries, stored_cache_keys, stored_cache_values, out_weight, lengths):
    n_blk, n_head = lax.axis_size("blk"), lax.axis_size("head")
    requests, span, kv_width = stored_cache_keys.shape
    group_width = QUERY_HEAD_COUNT // KEY_VALUE_HEADS
    local_heads = kv_width // HEAD_DIMENSION
    inputs, columns = out_weight.shape
    rows = requests * n_blk
    stack = group_width * rows
    width = columns // COLUMN_CHUNKS
    dims = (n_blk, n_head, requests, span, local_heads, group_width)
    hbm = pl.BlockSpec(memory_space=pl.ANY)
    parts = pl.pallas_call(
        functools.partial(fused_kernel, dims),
        out_shape=jax.ShapeDtypeStruct(
            (COLUMN_CHUNKS, n_head, requests, width), jnp.float32
        ),
        in_specs=[hbm] * 5,
        out_specs=hbm,
        scratch_shapes=[
            pltpu.SMEM((requests,), jnp.int32),
            pltpu.VMEM((n_blk, requests, inputs), jnp.bfloat16),
            pltpu.VMEM((requests * span, kv_width), jnp.bfloat16),
            pltpu.VMEM((requests * span, kv_width), jnp.bfloat16),
            pltpu.VMEM((inputs, columns), jnp.bfloat16),
            pltpu.VMEM((local_heads, n_blk, stack, HEAD_DIMENSION), jnp.bfloat16),
            pltpu.VMEM((local_heads, n_blk, 1, LANES), jnp.float32),
            pltpu.VMEM((rows, columns), jnp.float32),
            pltpu.VMEM((COLUMN_CHUNKS, n_head, requests, width), jnp.float32),
            pltpu.SemaphoreType.DMA((4,)),
            pltpu.SemaphoreType.DMA((local_heads,)),
            pltpu.SemaphoreType.DMA((n_blk,)),
            pltpu.SemaphoreType.DMA((n_blk,)),
            pltpu.SemaphoreType.DMA((local_heads, n_blk)),
            pltpu.SemaphoreType.DMA((local_heads, n_blk)),
            pltpu.SemaphoreType.DMA((local_heads, n_blk)),
            pltpu.SemaphoreType.DMA((local_heads, n_blk)),
            pltpu.SemaphoreType.DMA((COLUMN_CHUNKS, n_head)),
            pltpu.SemaphoreType.DMA((COLUMN_CHUNKS, n_head)),
        ],
        compiler_params=pltpu.CompilerParams(collective_id=0, has_side_effects=True),
    )(
        lengths,
        queries.reshape(requests, inputs),
        stored_cache_keys.reshape(requests * span, kv_width),
        stored_cache_values.reshape(requests * span, kv_width),
        out_weight,
    )
    summed = jnp.sum(parts, axis=1).astype(jnp.bfloat16)
    return summed.transpose(1, 0, 2).reshape(requests, 1, columns)


def layer(queries, stored_cache_keys, *others):
    tokens = queries.shape[1] * lax.axis_size("blk")
    fits = (
        queries.shape[1] == 1
        and tokens == lax.axis_size("head")
        and tokens * queries.shape[0] == 8
        and QUERY_HEAD_COUNT // KEY_VALUE_HEADS * 8 == LANES // 2
    )
    return (fused if fits else body)(queries, stored_cache_keys, *others)


def body(queries, stored_cache_keys, stored_cache_values, out_weight, lengths):
    group_width = QUERY_HEAD_COUNT // KEY_VALUE_HEADS
    local_heads = stored_cache_keys.shape[2] // HEAD_DIMENSION
    query_heads = local_heads * group_width
    span = stored_cache_keys.shape[1]
    new_count = queries.shape[1] * lax.axis_size("blk")
    key_pos = lax.axis_index("blk") * span + jnp.arange(span, dtype=jnp.int32)
    score_scale = 1.0 / math.sqrt(HEAD_DIMENSION)
    piece = lax.all_gather(queries, "blk", axis=1, tiled=True)
    rows_count = piece.shape[1]
    query_pos = lengths[:, None] - new_count + jnp.arange(rows_count, dtype=jnp.int32)[None, :]
    sums_list = []
    maxima_list = []
    totals_list = []
    for request in range(REQUEST_COUNT):
        visible = (key_pos[None, :] <= query_pos[request][:, None])[:, None, :]
        parts_sum, parts_max, parts_total = ([], [], [])
        for kv_head in range(local_heads):
            block_query = piece[
                request,
                :,
                kv_head
                * group_width
                * HEAD_DIMENSION : (kv_head + 1)
                * group_width
                * HEAD_DIMENSION,
            ].reshape(rows_count, group_width, HEAD_DIMENSION)
            local_keys = stored_cache_keys[
                request, :, kv_head * HEAD_DIMENSION : (kv_head + 1) * HEAD_DIMENSION
            ]
            local_values = stored_cache_values[
                request, :, kv_head * HEAD_DIMENSION : (kv_head + 1) * HEAD_DIMENSION
            ]
            scores = (
                jnp.einsum(
                    "ngd,cd->ngc", block_query, local_keys, preferred_element_type=jnp.float32
                )
                * score_scale
            )
            block_max = jnp.max(jnp.where(visible, scores, masked_fill_value), axis=-1)
            weights = jnp.where(visible, jnp.exp(scores - block_max[..., None]), 0.0)
            parts_total.append(jnp.sum(weights, axis=-1))
            parts_max.append(block_max)
            weighted = jnp.einsum(
                "ngc,cd->ngd",
                weights.astype(jnp.bfloat16),
                local_values,
                preferred_element_type=jnp.float32,
            )
            parts_sum.append(weighted.reshape(rows_count, group_width * HEAD_DIMENSION))
        sums_list.append(jnp.concatenate(parts_sum, axis=1))
        maxima_list.append(jnp.concatenate(parts_max, axis=1))
        totals_list.append(jnp.concatenate(parts_total, axis=1))
    new_sums = jnp.stack(sums_list, axis=0)
    new_maxima = jnp.stack(maxima_list, axis=0)
    new_totals = jnp.stack(totals_list, axis=0)
    received = (
        lax.all_to_all(new_sums[None], "blk", split_axis=2, concat_axis=0, tiled=True),
        lax.all_to_all(new_maxima[None], "blk", split_axis=2, concat_axis=0, tiled=True),
        lax.all_to_all(new_totals[None], "blk", split_axis=2, concat_axis=0, tiled=True),
    )
    part_sums, part_max, part_totals = received
    blocks = part_sums.shape[0]
    own_rows = part_sums.shape[2]
    top = jnp.max(part_max, axis=0)
    factor = jnp.exp(part_max - top[None])
    overall = jnp.sum(factor * part_totals, axis=0)
    shaped = part_sums.reshape(blocks, REQUEST_COUNT, own_rows, query_heads, HEAD_DIMENSION)
    merged = jnp.sum(shaped * factor[..., None], axis=0) / overall[..., None]
    own_attention = merged.astype(jnp.bfloat16).reshape(
        REQUEST_COUNT, own_rows, query_heads * HEAD_DIMENSION
    )
    terms = jnp.einsum(
        "rnc,cd->rnd",
        lax.all_gather(own_attention, "blk", axis=1, tiled=True),
        out_weight,
        preferred_element_type=jnp.float32,
    )
    return lax.psum_scatter(terms, "head", scatter_dimension=1, tiled=True).astype(jnp.bfloat16)


def solution(mesh):
    placed = (
        P("groups", "blk", "head"),
        P("groups", "blk", "head"),
        P("groups", "blk", "head"),
        P("head", "blk"),
        P("groups"),
    )
    return jax.shard_map(
        layer, mesh=mesh, in_specs=placed, out_specs=P("groups", "head", "blk"), check_vma=False
    )
```

```python
import functools
import math

import jax
import jax.numpy as jnp
from jax import lax
from jax.experimental import pallas as pl
from jax.experimental.pallas import tpu as pltpu
from jax.sharding import PartitionSpec as P

REQUEST_COUNT = 2
QUERY_HEAD_COUNT = 64
KEY_VALUE_HEADS = 8
HEAD_DIMENSION = 128


masked_fill_value = -1e30


MESH = pl.DeviceIdType.MESH
COLUMN_CHUNKS = 1
LANES = 128


def fused_kernel(
    dims,
    lengths_hbm,
    queries_hbm,
    keys_hbm,
    values_hbm,
    weight_hbm,
    parts_hbm,
    lengths_ref,
    query_slots,
    keys_ref,
    values_ref,
    weight_ref,
    sum_slots,
    stat_slots,
    acc_ref,
    terms_ref,
    local_sem,
    weight_sem,
    query_send,
    query_recv,
    sum_send,
    sum_recv,
    stat_send,
    stat_recv,
    term_send,
    term_recv,
):
    n_blk, n_head, requests, span, local_heads, group_width = dims
    my_blk = lax.axis_index("blk")
    my_head = lax.axis_index("head")
    rows = n_blk * requests
    stack = group_width * rows
    depth = group_width * HEAD_DIMENSION
    columns = weight_ref.shape[1]
    width = columns // COLUMN_CHUNKS

    barrier = pltpu.get_barrier_semaphore()
    for step in range(1, n_blk):
        peer = lax.rem(my_blk + step, n_blk)
        pl.semaphore_signal(barrier, inc=1, device_id={"blk": peer}, device_id_type=MESH)
    for step in range(1, n_head):
        peer = lax.rem(my_head + step, n_head)
        pl.semaphore_signal(barrier, inc=1, device_id={"head": peer}, device_id_type=MESH)
    query_copy = pltpu.make_async_copy(
        queries_hbm, query_slots.at[my_blk], local_sem.at[2]
    )
    query_copy.start()
    length_copy = pltpu.make_async_copy(lengths_hbm, lengths_ref, local_sem.at[3])
    length_copy.start()
    key_copy = pltpu.make_async_copy(keys_hbm, keys_ref, local_sem.at[0])
    value_copy = pltpu.make_async_copy(values_hbm, values_ref, local_sem.at[1])
    key_copy.start()
    value_copy.start()
    weight_copies = []
    for kv_head in range(local_heads):
        part = pl.ds(kv_head * depth, depth)
        weight_copies.append(
            pltpu.make_async_copy(
                weight_hbm.at[part], weight_ref.at[part], weight_sem.at[kv_head]
            )
        )
        weight_copies[-1].start()

    query_copy.wait()
    pl.semaphore_wait(barrier, n_blk + n_head - 2)

    peers = []
    for k in range(n_blk - 1):
        down = n_blk - 1 - k
        down = jnp.where(down <= my_blk, down - 1, down)
        up = jnp.where(k >= my_blk, k + 1, k)
        peers.append(jnp.where(my_blk < n_blk // 2, down, up))

    query_copies = []
    for peer in peers:
        copy = pltpu.make_async_remote_copy(
            src_ref=query_slots.at[my_blk],
            dst_ref=query_slots.at[my_blk],
            send_sem=query_send.at[peer],
            recv_sem=query_recv.at[my_blk],
            device_id={"blk": peer},
            device_id_type=MESH,
        )
        copy.start()
        query_copies.append(copy)
    length_copy.wait()

    row = lax.broadcasted_iota(jnp.int32, (rows, requests * span), 0)
    column = lax.broadcasted_iota(jnp.int32, (rows, requests * span), 1)
    token, row_request = row // requests, row % requests
    position = my_blk * span + column % span
    visible = jnp.zeros((rows, requests * span), jnp.bool_)
    for request in range(requests):
        here = (column // span == request) & (row_request == request)
        seen = position <= lengths_ref[request] - n_blk + token
        visible = visible | (here & seen)
    visible = visible[None]
    score_scale = 1.0 / math.sqrt(HEAD_DIMENSION)
    lane = lax.broadcasted_iota(jnp.int32, (stack, LANES), 1)
    own_lane = lax.broadcasted_iota(jnp.int32, (stack, LANES), 0)
    max_place, total_place = lane == own_lane, lane == own_lane + LANES // 2

    for peer, copy in zip(peers, query_copies):
        pltpu.make_async_copy(
            query_slots.at[peer], query_slots.at[peer], query_recv.at[peer]
        ).wait()
    gathered = jnp.concatenate(
        [query_slots[b].astype(jnp.float32) for b in range(n_blk)], axis=0
    )
    key_copy.wait()
    value_copy.wait()

    partial_copies = []
    for kv_head in range(local_heads):
        entries = pl.ds(kv_head * HEAD_DIMENSION, HEAD_DIMENSION)
        block_query = jnp.concatenate(
            [
                gathered[:, h * HEAD_DIMENSION : (h + 1) * HEAD_DIMENSION]
                for h in range(kv_head * group_width, (kv_head + 1) * group_width)
            ],
            axis=0,
        ).astype(jnp.bfloat16)
        scores = lax.dot_general(
            block_query,
            keys_ref[:, entries],
            (((1,), (1,)), ((), ())),
            preferred_element_type=jnp.float32,
        )
        scores = (scores * score_scale).reshape(group_width, rows, requests * span)
        block_max = jnp.max(
            jnp.where(visible, scores, masked_fill_value), axis=-1, keepdims=True
        )
        weights = jnp.where(visible, jnp.exp(scores - block_max), 0.0)
        total = jnp.sum(weights, axis=-1, keepdims=True)
        weighted = jnp.dot(
            weights.reshape(stack, requests * span).astype(jnp.bfloat16),
            values_ref[:, entries],
            preferred_element_type=jnp.float32,
        )
        sum_slots[kv_head, my_blk] = weighted.astype(sum_slots.dtype)
        stats = jnp.where(
            max_place,
            block_max.reshape(stack, 1),
            jnp.where(total_place, total.reshape(stack, 1), 0.0),
        )
        stat_slots[kv_head, my_blk] = jnp.sum(stats, axis=0, keepdims=True)
        copies = []
        for peer in peers:
            for slots, send, recv in (
                (stat_slots, stat_send, stat_recv),
                (sum_slots, sum_send, sum_recv),
            ):
                copy = pltpu.make_async_remote_copy(
                    src_ref=slots.at[kv_head, my_blk],
                    dst_ref=slots.at[kv_head, my_blk],
                    send_sem=send.at[kv_head, peer],
                    recv_sem=recv.at[kv_head, my_blk],
                    device_id={"blk": peer},
                    device_id_type=MESH,
                )
                copy.start()
                copies.append(copy)
        partial_copies.append(copies)

    term_copies = []
    for kv_head in range(local_heads):
        for peer in peers:
            for slots, recv in ((stat_slots, stat_recv), (sum_slots, sum_recv)):
                here = slots.at[kv_head, peer]
                pltpu.make_async_copy(here, here, recv.at[kv_head, peer]).wait()
        maxima = [stat_slots[kv_head, b] for b in range(n_blk)]
        totals = [pltpu.roll(x, LANES // 2, 1) for x in maxima]
        top = functools.reduce(jnp.maximum, maxima)
        factors = [jnp.exp(x - top) for x in maxima]
        overall = sum(f * x for f, x in zip(factors, totals))
        overall = jnp.where(lane[0:1] < stack, overall, 1.0)
        merged = jnp.zeros((stack, HEAD_DIMENSION), jnp.float32)
        for b in range(n_blk):
            share = jnp.sum(
                jnp.where(max_place, factors[b] / overall, 0.0), axis=1, keepdims=True
            )
            merged = merged + sum_slots[kv_head, b].astype(jnp.float32) * share
        attention = jnp.concatenate(
            [merged[g * rows : (g + 1) * rows] for g in range(group_width)], axis=1
        ).astype(jnp.bfloat16)
        weight_copies[kv_head].wait()
        part = pl.ds(kv_head * depth, depth)
        for chunk in range(COLUMN_CHUNKS):
            where = pl.ds(chunk * width, width)
            term = jnp.dot(
                attention, weight_ref[part, where], preferred_element_type=jnp.float32
            )
            if kv_head > 0:
                term = term + acc_ref[:, where]
            if kv_head < local_heads - 1:
                acc_ref[:, where] = term
                continue
            for h in range(n_head):
                terms_ref[chunk, h] = term[h * requests : (h + 1) * requests]
            own_copy = pltpu.make_async_copy(
                terms_ref.at[chunk, my_head],
                parts_hbm.at[chunk, my_head],
                term_send.at[chunk, 0],
            )
            own_copy.start()
            term_copies.append(own_copy)
            for step in range(1, n_head):
                peer = lax.rem(my_head + step, n_head)
                copy = pltpu.make_async_remote_copy(
                    src_ref=terms_ref.at[chunk, peer],
                    dst_ref=parts_hbm.at[chunk, my_head],
                    send_sem=term_send.at[chunk, step],
                    recv_sem=term_recv.at[chunk, step],
                    device_id={"head": peer},
                    device_id_type=MESH,
                )
                copy.start()
                term_copies.append(copy)

    for copy in term_copies:
        copy.wait()
    for copies in [query_copies] + partial_copies:
        for copy in copies:
            copy.wait_send()


def fused(queries, stored_cache_keys, stored_cache_values, out_weight, lengths):
    n_blk, n_head = lax.axis_size("blk"), lax.axis_size("head")
    requests, span, kv_width = stored_cache_keys.shape
    group_width = QUERY_HEAD_COUNT // KEY_VALUE_HEADS
    local_heads = kv_width // HEAD_DIMENSION
    inputs, columns = out_weight.shape
    rows = requests * n_blk
    stack = group_width * rows
    width = columns // COLUMN_CHUNKS
    dims = (n_blk, n_head, requests, span, local_heads, group_width)
    hbm = pl.BlockSpec(memory_space=pl.ANY)
    parts = pl.pallas_call(
        functools.partial(fused_kernel, dims),
        out_shape=jax.ShapeDtypeStruct(
            (COLUMN_CHUNKS, n_head, requests, width), jnp.float32
        ),
        in_specs=[hbm] * 5,
        out_specs=hbm,
        scratch_shapes=[
            pltpu.SMEM((requests,), jnp.int32),
            pltpu.VMEM((n_blk, requests, inputs), jnp.bfloat16),
            pltpu.VMEM((requests * span, kv_width), jnp.bfloat16),
            pltpu.VMEM((requests * span, kv_width), jnp.bfloat16),
            pltpu.VMEM((inputs, columns), jnp.bfloat16),
            pltpu.VMEM((local_heads, n_blk, stack, HEAD_DIMENSION), jnp.bfloat16),
            pltpu.VMEM((local_heads, n_blk, 1, LANES), jnp.float32),
            pltpu.VMEM((rows, columns), jnp.float32),
            pltpu.VMEM((COLUMN_CHUNKS, n_head, requests, width), jnp.float32),
            pltpu.SemaphoreType.DMA((4,)),
            pltpu.SemaphoreType.DMA((local_heads,)),
            pltpu.SemaphoreType.DMA((n_blk,)),
            pltpu.SemaphoreType.DMA((n_blk,)),
            pltpu.SemaphoreType.DMA((local_heads, n_blk)),
            pltpu.SemaphoreType.DMA((local_heads, n_blk)),
            pltpu.SemaphoreType.DMA((local_heads, n_blk)),
            pltpu.SemaphoreType.DMA((local_heads, n_blk)),
            pltpu.SemaphoreType.DMA((COLUMN_CHUNKS, n_head)),
            pltpu.SemaphoreType.DMA((COLUMN_CHUNKS, n_head)),
        ],
        compiler_params=pltpu.CompilerParams(collective_id=0, vmem_limit_bytes=32768 * 1024, has_side_effects=True),
    )(
        *(
            pltpu.with_memory_space_constraint(x, pltpu.HBM)
            for x in (
                lengths,
                queries.reshape(requests, inputs),
                stored_cache_keys.reshape(requests * span, kv_width),
                stored_cache_values.reshape(requests * span, kv_width),
                out_weight,
            )
        )
    )
    summed = jnp.sum(parts, axis=1).astype(jnp.bfloat16)
    return summed.transpose(1, 0, 2).reshape(requests, 1, columns)


def layer(queries, stored_cache_keys, *others):
    tokens = queries.shape[1] * lax.axis_size("blk")
    fits = (
        queries.shape[1] == 1
        and tokens == lax.axis_size("head")
        and tokens * queries.shape[0] == 8
        and QUERY_HEAD_COUNT // KEY_VALUE_HEADS * 8 == LANES // 2
    )
    return (fused if fits else body)(queries, stored_cache_keys, *others)


def body(queries, stored_cache_keys, stored_cache_values, out_weight, lengths):
    group_width = QUERY_HEAD_COUNT // KEY_VALUE_HEADS
    local_heads = stored_cache_keys.shape[2] // HEAD_DIMENSION
    query_heads = local_heads * group_width
    span = stored_cache_keys.shape[1]
    new_count = queries.shape[1] * lax.axis_size("blk")
    key_pos = lax.axis_index("blk") * span + jnp.arange(span, dtype=jnp.int32)
    score_scale = 1.0 / math.sqrt(HEAD_DIMENSION)
    piece = lax.all_gather(queries, "blk", axis=1, tiled=True)
    rows_count = piece.shape[1]
    query_pos = lengths[:, None] - new_count + jnp.arange(rows_count, dtype=jnp.int32)[None, :]
    sums_list = []
    maxima_list = []
    totals_list = []
    for request in range(REQUEST_COUNT):
        visible = (key_pos[None, :] <= query_pos[request][:, None])[:, None, :]
        parts_sum, parts_max, parts_total = ([], [], [])
        for kv_head in range(local_heads):
            block_query = piece[
                request,
                :,
                kv_head
                * group_width
                * HEAD_DIMENSION : (kv_head + 1)
                * group_width
                * HEAD_DIMENSION,
            ].reshape(rows_count, group_width, HEAD_DIMENSION)
            local_keys = stored_cache_keys[
                request, :, kv_head * HEAD_DIMENSION : (kv_head + 1) * HEAD_DIMENSION
            ]
            local_values = stored_cache_values[
                request, :, kv_head * HEAD_DIMENSION : (kv_head + 1) * HEAD_DIMENSION
            ]
            scores = (
                jnp.einsum(
                    "ngd,cd->ngc", block_query, local_keys, preferred_element_type=jnp.float32
                )
                * score_scale
            )
            block_max = jnp.max(jnp.where(visible, scores, masked_fill_value), axis=-1)
            weights = jnp.where(visible, jnp.exp(scores - block_max[..., None]), 0.0)
            parts_total.append(jnp.sum(weights, axis=-1))
            parts_max.append(block_max)
            weighted = jnp.einsum(
                "ngc,cd->ngd",
                weights.astype(jnp.bfloat16),
                local_values,
                preferred_element_type=jnp.float32,
            )
            parts_sum.append(weighted.reshape(rows_count, group_width * HEAD_DIMENSION))
        sums_list.append(jnp.concatenate(parts_sum, axis=1))
        maxima_list.append(jnp.concatenate(parts_max, axis=1))
        totals_list.append(jnp.concatenate(parts_total, axis=1))
    new_sums = jnp.stack(sums_list, axis=0)
    new_maxima = jnp.stack(maxima_list, axis=0)
    new_totals = jnp.stack(totals_list, axis=0)
    received = (
        lax.all_to_all(new_sums[None], "blk", split_axis=2, concat_axis=0, tiled=True),
        lax.all_to_all(new_maxima[None], "blk", split_axis=2, concat_axis=0, tiled=True),
        lax.all_to_all(new_totals[None], "blk", split_axis=2, concat_axis=0, tiled=True),
    )
    part_sums, part_max, part_totals = received
    blocks = part_sums.shape[0]
    own_rows = part_sums.shape[2]
    top = jnp.max(part_max, axis=0)
    factor = jnp.exp(part_max - top[None])
    overall = jnp.sum(factor * part_totals, axis=0)
    shaped = part_sums.reshape(blocks, REQUEST_COUNT, own_rows, query_heads, HEAD_DIMENSION)
    merged = jnp.sum(shaped * factor[..., None], axis=0) / overall[..., None]
    own_attention = merged.astype(jnp.bfloat16).reshape(
        REQUEST_COUNT, own_rows, query_heads * HEAD_DIMENSION
    )
    terms = jnp.einsum(
        "rnc,cd->rnd",
        lax.all_gather(own_attention, "blk", axis=1, tiled=True),
        out_weight,
        preferred_element_type=jnp.float32,
    )
    return lax.psum_scatter(terms, "head", scatter_dimension=1, tiled=True).astype(jnp.bfloat16)


def solution(mesh):
    placed = (
        P("groups", "blk", "head"),
        P("groups", "blk", "head"),
        P("groups", "blk", "head"),
        P("head", "blk"),
        P("groups"),
    )
    return jax.shard_map(
        layer, mesh=mesh, in_specs=placed, out_specs=P("groups", "head", "blk"), check_vma=False
    )
```

```python
import functools
import math

import jax
import jax.numpy as jnp
from jax import lax
from jax.experimental import pallas as pl
from jax.experimental.pallas import tpu as pltpu
from jax.sharding import PartitionSpec as P

REQUEST_COUNT = 2
QUERY_HEAD_COUNT = 64
KEY_VALUE_HEADS = 8
HEAD_DIMENSION = 128


masked_fill_value = -1e30


MESH = pl.DeviceIdType.MESH
COLUMN_CHUNKS = 1
LANES = 128
TILE_ROWS = 16
PARTS = 3


def fused_kernel(
    dims,
    lengths_hbm,
    queries_hbm,
    keys_hbm,
    values_hbm,
    weight_hbm,
    parts_hbm,
    lengths_ref,
    query_slots,
    keys_ref,
    values_ref,
    weight_ref,
    sum_slots,
    acc_ref,
    terms_ref,
    local_sem,
    weight_sem,
    query_send,
    query_recv,
    sum_send,
    sum_recv,
    term_send,
    term_recv,
):
    n_blk, n_head, requests, span, local_heads, group_width = dims
    my_blk = lax.axis_index("blk")
    my_head = lax.axis_index("head")
    rows = n_blk * requests
    stack = group_width * rows
    depth = group_width * HEAD_DIMENSION
    columns = weight_ref.shape[1]
    width = columns // COLUMN_CHUNKS

    barrier = pltpu.get_barrier_semaphore()
    for step in range(1, n_blk):
        peer = lax.rem(my_blk + step, n_blk)
        pl.semaphore_signal(barrier, inc=1, device_id={"blk": peer}, device_id_type=MESH)
    for step in range(1, n_head):
        peer = lax.rem(my_head + step, n_head)
        pl.semaphore_signal(barrier, inc=1, device_id={"head": peer}, device_id_type=MESH)
    query_copy = pltpu.make_async_copy(
        queries_hbm, query_slots.at[my_blk], local_sem.at[2]
    )
    query_copy.start()
    length_copy = pltpu.make_async_copy(lengths_hbm, lengths_ref, local_sem.at[3])
    length_copy.start()
    key_copy = pltpu.make_async_copy(keys_hbm, keys_ref, local_sem.at[0])
    value_copy = pltpu.make_async_copy(values_hbm, values_ref, local_sem.at[1])
    key_copy.start()
    value_copy.start()
    weight_copies = []
    for kv_head in range(local_heads):
        part = pl.ds(kv_head * depth, depth)
        weight_copies.append(
            pltpu.make_async_copy(
                weight_hbm.at[part], weight_ref.at[part], weight_sem.at[kv_head]
            )
        )
        weight_copies[-1].start()

    query_copy.wait()
    pl.semaphore_wait(barrier, n_blk + n_head - 2)

    peers = []
    for k in range(n_blk - 1):
        down = n_blk - 1 - k
        down = jnp.where(down <= my_blk, down - 1, down)
        up = jnp.where(k >= my_blk, k + 1, k)
        peers.append(jnp.where(my_blk < n_blk // 2, down, up))

    query_copies = []
    for peer in peers:
        copy = pltpu.make_async_remote_copy(
            src_ref=query_slots.at[my_blk],
            dst_ref=query_slots.at[my_blk],
            send_sem=query_send.at[peer],
            recv_sem=query_recv.at[my_blk],
            device_id={"blk": peer},
            device_id_type=MESH,
        )
        copy.start()
        query_copies.append(copy)
    length_copy.wait()

    row = lax.broadcasted_iota(jnp.int32, (rows, requests * span), 0)
    column = lax.broadcasted_iota(jnp.int32, (rows, requests * span), 1)
    token, row_request = row // requests, row % requests
    position = my_blk * span + column % span
    visible = jnp.zeros((rows, requests * span), jnp.bool_)
    for request in range(requests):
        here = (column // span == request) & (row_request == request)
        seen = position <= lengths_ref[request] - n_blk + token
        visible = visible | (here & seen)
    visible = visible[None]
    score_scale = 1.0 / math.sqrt(HEAD_DIMENSION)
    lane = lax.broadcasted_iota(jnp.int32, (stack, LANES), 1)
    own_lane = lax.broadcasted_iota(jnp.int32, (stack, LANES), 0)
    max_place, total_place = lane == own_lane, lane == own_lane + LANES // 2

    key_copy.wait()
    value_copy.wait()
    for peer in peers:
        pltpu.make_async_copy(
            query_slots.at[peer], query_slots.at[peer], query_recv.at[peer]
        ).wait()
    gathered = jnp.concatenate(
        [query_slots[b].astype(jnp.float32) for b in range(n_blk)], axis=0
    )

    partial_copies = []
    for kv_head in range(local_heads):
        entries = pl.ds(kv_head * HEAD_DIMENSION, HEAD_DIMENSION)
        block_query = jnp.concatenate(
            [
                gathered[:, h * HEAD_DIMENSION : (h + 1) * HEAD_DIMENSION]
                for h in range(kv_head * group_width, (kv_head + 1) * group_width)
            ],
            axis=0,
        ).astype(jnp.bfloat16)
        scores = lax.dot_general(
            block_query,
            keys_ref[:, entries],
            (((1,), (1,)), ((), ())),
            preferred_element_type=jnp.float32,
        )
        scores = (scores * score_scale).reshape(group_width, rows, requests * span)
        block_max = jnp.max(
            jnp.where(visible, scores, masked_fill_value), axis=-1, keepdims=True
        )
        weights = jnp.where(visible, jnp.exp(scores - block_max), 0.0)
        total = jnp.sum(weights, axis=-1, keepdims=True)
        weighted = jnp.dot(
            weights.reshape(stack, requests * span).astype(jnp.bfloat16),
            values_ref[:, entries],
            preferred_element_type=jnp.float32,
        )
        stats = jnp.where(
            max_place,
            block_max.reshape(stack, 1),
            jnp.where(total_place, total.reshape(stack, 1), 0.0),
        )
        rest = jnp.sum(stats, axis=0, keepdims=True)
        parts = []
        for _ in range(PARTS):
            parts.append(rest.astype(jnp.bfloat16).astype(jnp.float32))
            rest = rest - parts[-1]
        parts.append(jnp.zeros((TILE_ROWS - PARTS, LANES), jnp.float32))
        sum_slots[kv_head, my_blk] = jnp.concatenate(
            [weighted] + parts, axis=0
        ).astype(jnp.bfloat16)
        copies = []
        for peer in peers:
            copy = pltpu.make_async_remote_copy(
                src_ref=sum_slots.at[kv_head, my_blk],
                dst_ref=sum_slots.at[kv_head, my_blk],
                send_sem=sum_send.at[kv_head, peer],
                recv_sem=sum_recv.at[kv_head, my_blk],
                device_id={"blk": peer},
                device_id_type=MESH,
            )
            copy.start()
            copies.append(copy)
        partial_copies.append(copies)

    for copy in weight_copies:
        copy.wait()
    term_copies = []
    for kv_head in range(local_heads):
        for peer in peers:
            here = sum_slots.at[kv_head, peer]
            pltpu.make_async_copy(here, here, sum_recv.at[kv_head, peer]).wait()
        slots = [sum_slots[kv_head, b].astype(jnp.float32) for b in range(n_blk)]
        maxima = [
            sum(x[stack + i : stack + i + 1] for i in range(PARTS)) for x in slots
        ]
        totals = [pltpu.roll(x, LANES // 2, 1) for x in maxima]
        top = functools.reduce(jnp.maximum, maxima)
        factors = [jnp.exp(x - top) for x in maxima]
        overall = sum(f * x for f, x in zip(factors, totals))
        overall = jnp.where(lane[0:1] < stack, overall, 1.0)
        merged = jnp.zeros((stack, HEAD_DIMENSION), jnp.float32)
        for b in range(n_blk):
            share = jnp.sum(
                jnp.where(max_place, factors[b] / overall, 0.0), axis=1, keepdims=True
            )
            merged = merged + slots[b][:stack] * share
        attention = jnp.concatenate(
            [merged[g * rows : (g + 1) * rows] for g in range(group_width)], axis=1
        ).astype(jnp.bfloat16)
        part = pl.ds(kv_head * depth, depth)
        for chunk in range(COLUMN_CHUNKS):
            where = pl.ds(chunk * width, width)
            term = jnp.dot(
                attention, weight_ref[part, where], preferred_element_type=jnp.float32
            )
            if kv_head > 0:
                term = term + acc_ref[:, where]
            if kv_head < local_heads - 1:
                acc_ref[:, where] = term
                continue
            for h in range(n_head):
                terms_ref[chunk, h] = term[h * requests : (h + 1) * requests]
            for step in range(1, n_head):
                peer = lax.rem(my_head + step, n_head)
                copy = pltpu.make_async_remote_copy(
                    src_ref=terms_ref.at[chunk, peer],
                    dst_ref=parts_hbm.at[chunk, my_head],
                    send_sem=term_send.at[chunk, step],
                    recv_sem=term_recv.at[chunk, step],
                    device_id={"head": peer},
                    device_id_type=MESH,
                )
                copy.start()
                term_copies.append(copy)
            own_copy = pltpu.make_async_copy(
                terms_ref.at[chunk, my_head],
                parts_hbm.at[chunk, my_head],
                term_send.at[chunk, 0],
            )
            own_copy.start()
            term_copies.append(own_copy)

    for copies in [query_copies] + partial_copies:
        for copy in copies:
            copy.wait_send()
    for copy in term_copies:
        copy.wait()


def fused(queries, stored_cache_keys, stored_cache_values, out_weight, lengths):
    n_blk, n_head = lax.axis_size("blk"), lax.axis_size("head")
    requests, span, kv_width = stored_cache_keys.shape
    group_width = QUERY_HEAD_COUNT // KEY_VALUE_HEADS
    local_heads = kv_width // HEAD_DIMENSION
    inputs, columns = out_weight.shape
    rows = requests * n_blk
    stack = group_width * rows
    width = columns // COLUMN_CHUNKS
    dims = (n_blk, n_head, requests, span, local_heads, group_width)
    hbm = pl.BlockSpec(memory_space=pl.ANY)
    parts = pl.pallas_call(
        functools.partial(fused_kernel, dims),
        out_shape=jax.ShapeDtypeStruct(
            (COLUMN_CHUNKS, n_head, requests, width), jnp.float32
        ),
        in_specs=[hbm] * 5,
        out_specs=hbm,
        scratch_shapes=[
            pltpu.SMEM((requests,), jnp.int32),
            pltpu.VMEM((n_blk, requests, inputs), jnp.bfloat16),
            pltpu.VMEM((requests * span, kv_width), jnp.bfloat16),
            pltpu.VMEM((requests * span, kv_width), jnp.bfloat16),
            pltpu.VMEM((inputs, columns), jnp.bfloat16),
            pltpu.VMEM(
                (local_heads, n_blk, stack + TILE_ROWS, HEAD_DIMENSION), jnp.bfloat16
            ),
            pltpu.VMEM((rows, columns), jnp.float32),
            pltpu.VMEM((COLUMN_CHUNKS, n_head, requests, width), jnp.float32),
            pltpu.SemaphoreType.DMA((4,)),
            pltpu.SemaphoreType.DMA((local_heads,)),
            pltpu.SemaphoreType.DMA((n_blk,)),
            pltpu.SemaphoreType.DMA((n_blk,)),
            pltpu.SemaphoreType.DMA((local_heads, n_blk)),
            pltpu.SemaphoreType.DMA((local_heads, n_blk)),
            pltpu.SemaphoreType.DMA((COLUMN_CHUNKS, n_head)),
            pltpu.SemaphoreType.DMA((COLUMN_CHUNKS, n_head)),
        ],
        compiler_params=pltpu.CompilerParams(collective_id=0, vmem_limit_bytes=32768 * 1024, has_side_effects=True),
    )(
        *(
            pltpu.with_memory_space_constraint(x, pltpu.HBM)
            for x in (
                lengths,
                queries.reshape(requests, inputs),
                stored_cache_keys.reshape(requests * span, kv_width),
                stored_cache_values.reshape(requests * span, kv_width),
                out_weight,
            )
        )
    )
    summed = jnp.sum(parts, axis=1).astype(jnp.bfloat16)
    return summed.transpose(1, 0, 2).reshape(requests, 1, columns)


def layer(queries, stored_cache_keys, *others):
    tokens = queries.shape[1] * lax.axis_size("blk")
    fits = (
        queries.shape[1] == 1
        and tokens == lax.axis_size("head")
        and tokens * queries.shape[0] == 8
        and QUERY_HEAD_COUNT // KEY_VALUE_HEADS * 8 == LANES // 2
    )
    return (fused if fits else body)(queries, stored_cache_keys, *others)


def body(queries, stored_cache_keys, stored_cache_values, out_weight, lengths):
    group_width = QUERY_HEAD_COUNT // KEY_VALUE_HEADS
    local_heads = stored_cache_keys.shape[2] // HEAD_DIMENSION
    query_heads = local_heads * group_width
    span = stored_cache_keys.shape[1]
    new_count = queries.shape[1] * lax.axis_size("blk")
    key_pos = lax.axis_index("blk") * span + jnp.arange(span, dtype=jnp.int32)
    score_scale = 1.0 / math.sqrt(HEAD_DIMENSION)
    piece = lax.all_gather(queries, "blk", axis=1, tiled=True)
    rows_count = piece.shape[1]
    query_pos = lengths[:, None] - new_count + jnp.arange(rows_count, dtype=jnp.int32)[None, :]
    sums_list = []
    maxima_list = []
    totals_list = []
    for request in range(REQUEST_COUNT):
        visible = (key_pos[None, :] <= query_pos[request][:, None])[:, None, :]
        parts_sum, parts_max, parts_total = ([], [], [])
        for kv_head in range(local_heads):
            block_query = piece[
                request,
                :,
                kv_head
                * group_width
                * HEAD_DIMENSION : (kv_head + 1)
                * group_width
                * HEAD_DIMENSION,
            ].reshape(rows_count, group_width, HEAD_DIMENSION)
            local_keys = stored_cache_keys[
                request, :, kv_head * HEAD_DIMENSION : (kv_head + 1) * HEAD_DIMENSION
            ]
            local_values = stored_cache_values[
                request, :, kv_head * HEAD_DIMENSION : (kv_head + 1) * HEAD_DIMENSION
            ]
            scores = (
                jnp.einsum(
                    "ngd,cd->ngc", block_query, local_keys, preferred_element_type=jnp.float32
                )
                * score_scale
            )
            block_max = jnp.max(jnp.where(visible, scores, masked_fill_value), axis=-1)
            weights = jnp.where(visible, jnp.exp(scores - block_max[..., None]), 0.0)
            parts_total.append(jnp.sum(weights, axis=-1))
            parts_max.append(block_max)
            weighted = jnp.einsum(
                "ngc,cd->ngd",
                weights.astype(jnp.bfloat16),
                local_values,
                preferred_element_type=jnp.float32,
            )
            parts_sum.append(weighted.reshape(rows_count, group_width * HEAD_DIMENSION))
        sums_list.append(jnp.concatenate(parts_sum, axis=1))
        maxima_list.append(jnp.concatenate(parts_max, axis=1))
        totals_list.append(jnp.concatenate(parts_total, axis=1))
    new_sums = jnp.stack(sums_list, axis=0)
    new_maxima = jnp.stack(maxima_list, axis=0)
    new_totals = jnp.stack(totals_list, axis=0)
    received = (
        lax.all_to_all(new_sums[None], "blk", split_axis=2, concat_axis=0, tiled=True),
        lax.all_to_all(new_maxima[None], "blk", split_axis=2, concat_axis=0, tiled=True),
        lax.all_to_all(new_totals[None], "blk", split_axis=2, concat_axis=0, tiled=True),
    )
    part_sums, part_max, part_totals = received
    blocks = part_sums.shape[0]
    own_rows = part_sums.shape[2]
    top = jnp.max(part_max, axis=0)
    factor = jnp.exp(part_max - top[None])
    overall = jnp.sum(factor * part_totals, axis=0)
    shaped = part_sums.reshape(blocks, REQUEST_COUNT, own_rows, query_heads, HEAD_DIMENSION)
    merged = jnp.sum(shaped * factor[..., None], axis=0) / overall[..., None]
    own_attention = merged.astype(jnp.bfloat16).reshape(
        REQUEST_COUNT, own_rows, query_heads * HEAD_DIMENSION
    )
    terms = jnp.einsum(
        "rnc,cd->rnd",
        lax.all_gather(own_attention, "blk", axis=1, tiled=True),
        out_weight,
        preferred_element_type=jnp.float32,
    )
    return lax.psum_scatter(terms, "head", scatter_dimension=1, tiled=True).astype(jnp.bfloat16)


def solution(mesh):
    placed = (
        P("groups", "blk", "head"),
        P("groups", "blk", "head"),
        P("groups", "blk", "head"),
        P("head", "blk"),
        P("groups"),
    )
    return jax.shard_map(
        layer, mesh=mesh, in_specs=placed, out_specs=P("groups", "head", "blk"), check_vma=False
    )
```

```python
import functools
import math

import jax
import jax.numpy as jnp
from jax import lax
from jax.experimental import pallas as pl
from jax.experimental.pallas import tpu as pltpu
from jax.sharding import PartitionSpec as P

REQUEST_COUNT = 2
QUERY_HEAD_COUNT = 64
KEY_VALUE_HEADS = 8
HEAD_DIMENSION = 128


masked_fill_value = -1e30


MESH = pl.DeviceIdType.MESH
COLUMN_CHUNKS = 1
LANES = 128
TILE_ROWS = 16
PARTS = 3


def fused_kernel(
    dims,
    lengths_hbm,
    queries_hbm,
    keys_hbm,
    values_hbm,
    weight_hbm,
    parts_ref,
    lengths_ref,
    query_slots,
    keys_ref,
    values_ref,
    weight_ref,
    sum_slots,
    acc_ref,
    terms_ref,
    local_sem,
    weight_sem,
    query_send,
    query_recv,
    sum_send,
    sum_recv,
    term_send,
    term_recv,
):
    n_blk, n_head, requests, span, local_heads, group_width = dims
    my_blk = lax.axis_index("blk")
    my_head = lax.axis_index("head")
    rows = n_blk * requests
    stack = group_width * rows
    depth = group_width * HEAD_DIMENSION
    columns = weight_ref.shape[1]
    width = columns // COLUMN_CHUNKS

    barrier = pltpu.get_barrier_semaphore()
    for step in range(1, n_blk):
        peer = lax.rem(my_blk + step, n_blk)
        pl.semaphore_signal(barrier, inc=1, device_id={"blk": peer}, device_id_type=MESH)
    for step in range(1, n_head):
        peer = lax.rem(my_head + step, n_head)
        pl.semaphore_signal(barrier, inc=1, device_id={"head": peer}, device_id_type=MESH)
    query_copy = pltpu.make_async_copy(
        queries_hbm, query_slots.at[my_blk], local_sem.at[2]
    )
    query_copy.start()
    length_copy = pltpu.make_async_copy(lengths_hbm, lengths_ref, local_sem.at[3])
    length_copy.start()
    key_copy = pltpu.make_async_copy(keys_hbm, keys_ref, local_sem.at[0])
    value_copy = pltpu.make_async_copy(values_hbm, values_ref, local_sem.at[1])
    key_copy.start()
    value_copy.start()
    weight_copies = []
    for kv_head in range(local_heads):
        part = pl.ds(kv_head * depth, depth)
        weight_copies.append(
            pltpu.make_async_copy(
                weight_hbm.at[part], weight_ref.at[part], weight_sem.at[kv_head]
            )
        )
        weight_copies[-1].start()

    query_copy.wait()
    pl.semaphore_wait(barrier, n_blk + n_head - 2)

    peers = []
    for k in range(n_blk - 1):
        down = n_blk - 1 - k
        down = jnp.where(down <= my_blk, down - 1, down)
        up = jnp.where(k >= my_blk, k + 1, k)
        peers.append(jnp.where(my_blk < n_blk // 2, down, up))

    query_copies = []
    for peer in peers:
        copy = pltpu.make_async_remote_copy(
            src_ref=query_slots.at[my_blk],
            dst_ref=query_slots.at[my_blk],
            send_sem=query_send.at[peer],
            recv_sem=query_recv.at[my_blk],
            device_id={"blk": peer},
            device_id_type=MESH,
        )
        copy.start()
        query_copies.append(copy)
    length_copy.wait()

    row = lax.broadcasted_iota(jnp.int32, (rows, requests * span), 0)
    column = lax.broadcasted_iota(jnp.int32, (rows, requests * span), 1)
    token, row_request = row // requests, row % requests
    position = my_blk * span + column % span
    visible = jnp.zeros((rows, requests * span), jnp.bool_)
    for request in range(requests):
        here = (column // span == request) & (row_request == request)
        seen = position <= lengths_ref[request] - n_blk + token
        visible = visible | (here & seen)
    visible = visible[None]
    score_scale = 1.0 / math.sqrt(HEAD_DIMENSION)
    lane = lax.broadcasted_iota(jnp.int32, (stack, LANES), 1)
    own_lane = lax.broadcasted_iota(jnp.int32, (stack, LANES), 0)
    max_place, total_place = lane == own_lane, lane == own_lane + LANES // 2

    key_copy.wait()
    value_copy.wait()
    for peer in peers:
        pltpu.make_async_copy(
            query_slots.at[peer], query_slots.at[peer], query_recv.at[peer]
        ).wait()
    gathered = jnp.concatenate(
        [query_slots[b].astype(jnp.float32) for b in range(n_blk)], axis=0
    )

    partial_copies = []
    for kv_head in range(local_heads):
        entries = pl.ds(kv_head * HEAD_DIMENSION, HEAD_DIMENSION)
        block_query = jnp.concatenate(
            [
                gathered[:, h * HEAD_DIMENSION : (h + 1) * HEAD_DIMENSION]
                for h in range(kv_head * group_width, (kv_head + 1) * group_width)
            ],
            axis=0,
        ).astype(jnp.bfloat16)
        scores = lax.dot_general(
            block_query,
            keys_ref[:, entries],
            (((1,), (1,)), ((), ())),
            preferred_element_type=jnp.float32,
        )
        scores = (scores * score_scale).reshape(group_width, rows, requests * span)
        block_max = jnp.max(
            jnp.where(visible, scores, masked_fill_value), axis=-1, keepdims=True
        )
        weights = jnp.where(visible, jnp.exp(scores - block_max), 0.0)
        total = jnp.sum(weights, axis=-1, keepdims=True)
        weighted = jnp.dot(
            weights.reshape(stack, requests * span).astype(jnp.bfloat16),
            values_ref[:, entries],
            preferred_element_type=jnp.float32,
        )
        stats = jnp.where(
            max_place,
            block_max.reshape(stack, 1),
            jnp.where(total_place, total.reshape(stack, 1), 0.0),
        )
        rest = jnp.sum(stats, axis=0, keepdims=True)
        parts = []
        for _ in range(PARTS):
            parts.append(rest.astype(jnp.bfloat16).astype(jnp.float32))
            rest = rest - parts[-1]
        parts.append(jnp.zeros((TILE_ROWS - PARTS, LANES), jnp.float32))
        sum_slots[kv_head, my_blk] = jnp.concatenate(
            [weighted] + parts, axis=0
        ).astype(jnp.bfloat16)
        copies = []
        for peer in peers:
            copy = pltpu.make_async_remote_copy(
                src_ref=sum_slots.at[kv_head, my_blk],
                dst_ref=sum_slots.at[kv_head, my_blk],
                send_sem=sum_send.at[kv_head, peer],
                recv_sem=sum_recv.at[kv_head, my_blk],
                device_id={"blk": peer},
                device_id_type=MESH,
            )
            copy.start()
            copies.append(copy)
        partial_copies.append(copies)

    for copy in weight_copies:
        copy.wait()
    term_copies = []
    for kv_head in range(local_heads):
        for peer in peers:
            here = sum_slots.at[kv_head, peer]
            pltpu.make_async_copy(here, here, sum_recv.at[kv_head, peer]).wait()
        slots = [sum_slots[kv_head, b].astype(jnp.float32) for b in range(n_blk)]
        maxima = [
            sum(x[stack + i : stack + i + 1] for i in range(PARTS)) for x in slots
        ]
        totals = [pltpu.roll(x, LANES // 2, 1) for x in maxima]
        top = functools.reduce(jnp.maximum, maxima)
        factors = [jnp.exp(x - top) for x in maxima]
        overall = sum(f * x for f, x in zip(factors, totals))
        overall = jnp.where(lane[0:1] < stack, overall, 1.0)
        merged = jnp.zeros((stack, HEAD_DIMENSION), jnp.float32)
        for b in range(n_blk):
            share = jnp.sum(
                jnp.where(max_place, factors[b] / overall, 0.0), axis=1, keepdims=True
            )
            merged = merged + slots[b][:stack] * share
        attention = jnp.concatenate(
            [merged[g * rows : (g + 1) * rows] for g in range(group_width)], axis=1
        ).astype(jnp.bfloat16)
        part = pl.ds(kv_head * depth, depth)
        for chunk in range(COLUMN_CHUNKS):
            where = pl.ds(chunk * width, width)
            term = jnp.dot(
                attention, weight_ref[part, where], preferred_element_type=jnp.float32
            )
            if kv_head > 0:
                term = term + acc_ref[:, where]
            if kv_head < local_heads - 1:
                acc_ref[:, where] = term
                continue
            for h in range(n_head):
                terms_ref[chunk, h] = term[h * requests : (h + 1) * requests]
            for step in range(1, n_head):
                peer = lax.rem(my_head + step, n_head)
                copy = pltpu.make_async_remote_copy(
                    src_ref=terms_ref.at[chunk, peer],
                    dst_ref=parts_ref.at[chunk, my_head],
                    send_sem=term_send.at[chunk, step],
                    recv_sem=term_recv.at[chunk, step],
                    device_id={"head": peer},
                    device_id_type=MESH,
                )
                copy.start()
                term_copies.append(copy)
            parts_ref[chunk, my_head] = terms_ref[chunk, my_head]

    for copies in [query_copies] + partial_copies:
        for copy in copies:
            copy.wait_send()
    for copy in term_copies:
        copy.wait()


def fused(queries, stored_cache_keys, stored_cache_values, out_weight, lengths):
    n_blk, n_head = lax.axis_size("blk"), lax.axis_size("head")
    requests, span, kv_width = stored_cache_keys.shape
    group_width = QUERY_HEAD_COUNT // KEY_VALUE_HEADS
    local_heads = kv_width // HEAD_DIMENSION
    inputs, columns = out_weight.shape
    rows = requests * n_blk
    stack = group_width * rows
    width = columns // COLUMN_CHUNKS
    dims = (n_blk, n_head, requests, span, local_heads, group_width)
    hbm = pl.BlockSpec(memory_space=pl.ANY)
    parts = pl.pallas_call(
        functools.partial(fused_kernel, dims),
        out_shape=jax.ShapeDtypeStruct(
            (COLUMN_CHUNKS, n_head, requests, width), jnp.float32
        ),
        in_specs=[hbm] * 5,
        out_specs=pl.BlockSpec(memory_space=pltpu.VMEM),
        scratch_shapes=[
            pltpu.SMEM((requests,), jnp.int32),
            pltpu.VMEM((n_blk, requests, inputs), jnp.bfloat16),
            pltpu.VMEM((requests * span, kv_width), jnp.bfloat16),
            pltpu.VMEM((requests * span, kv_width), jnp.bfloat16),
            pltpu.VMEM((inputs, columns), jnp.bfloat16),
            pltpu.VMEM(
                (local_heads, n_blk, stack + TILE_ROWS, HEAD_DIMENSION), jnp.bfloat16
            ),
            pltpu.VMEM((rows, columns), jnp.float32),
            pltpu.VMEM((COLUMN_CHUNKS, n_head, requests, width), jnp.float32),
            pltpu.SemaphoreType.DMA((4,)),
            pltpu.SemaphoreType.DMA((local_heads,)),
            pltpu.SemaphoreType.DMA((n_blk,)),
            pltpu.SemaphoreType.DMA((n_blk,)),
            pltpu.SemaphoreType.DMA((local_heads, n_blk)),
            pltpu.SemaphoreType.DMA((local_heads, n_blk)),
            pltpu.SemaphoreType.DMA((COLUMN_CHUNKS, n_head)),
            pltpu.SemaphoreType.DMA((COLUMN_CHUNKS, n_head)),
        ],
        compiler_params=pltpu.CompilerParams(collective_id=0, vmem_limit_bytes=32768 * 1024, has_side_effects=True),
    )(
        *(
            pltpu.with_memory_space_constraint(x, pltpu.HBM)
            for x in (
                lengths,
                queries.reshape(requests, inputs),
                stored_cache_keys.reshape(requests * span, kv_width),
                stored_cache_values.reshape(requests * span, kv_width),
                out_weight,
            )
        )
    )
    summed = jnp.sum(parts, axis=1).astype(jnp.bfloat16)
    return summed.transpose(1, 0, 2).reshape(requests, 1, columns)


def layer(queries, stored_cache_keys, *others):
    tokens = queries.shape[1] * lax.axis_size("blk")
    fits = (
        queries.shape[1] == 1
        and tokens == lax.axis_size("head")
        and tokens * queries.shape[0] == 8
        and QUERY_HEAD_COUNT // KEY_VALUE_HEADS * 8 == LANES // 2
    )
    return (fused if fits else body)(queries, stored_cache_keys, *others)


def body(queries, stored_cache_keys, stored_cache_values, out_weight, lengths):
    group_width = QUERY_HEAD_COUNT // KEY_VALUE_HEADS
    local_heads = stored_cache_keys.shape[2] // HEAD_DIMENSION
    query_heads = local_heads * group_width
    span = stored_cache_keys.shape[1]
    new_count = queries.shape[1] * lax.axis_size("blk")
    key_pos = lax.axis_index("blk") * span + jnp.arange(span, dtype=jnp.int32)
    score_scale = 1.0 / math.sqrt(HEAD_DIMENSION)
    piece = lax.all_gather(queries, "blk", axis=1, tiled=True)
    rows_count = piece.shape[1]
    query_pos = lengths[:, None] - new_count + jnp.arange(rows_count, dtype=jnp.int32)[None, :]
    sums_list = []
    maxima_list = []
    totals_list = []
    for request in range(REQUEST_COUNT):
        visible = (key_pos[None, :] <= query_pos[request][:, None])[:, None, :]
        parts_sum, parts_max, parts_total = ([], [], [])
        for kv_head in range(local_heads):
            block_query = piece[
                request,
                :,
                kv_head
                * group_width
                * HEAD_DIMENSION : (kv_head + 1)
                * group_width
                * HEAD_DIMENSION,
            ].reshape(rows_count, group_width, HEAD_DIMENSION)
            local_keys = stored_cache_keys[
                request, :, kv_head * HEAD_DIMENSION : (kv_head + 1) * HEAD_DIMENSION
            ]
            local_values = stored_cache_values[
                request, :, kv_head * HEAD_DIMENSION : (kv_head + 1) * HEAD_DIMENSION
            ]
            scores = (
                jnp.einsum(
                    "ngd,cd->ngc", block_query, local_keys, preferred_element_type=jnp.float32
                )
                * score_scale
            )
            block_max = jnp.max(jnp.where(visible, scores, masked_fill_value), axis=-1)
            weights = jnp.where(visible, jnp.exp(scores - block_max[..., None]), 0.0)
            parts_total.append(jnp.sum(weights, axis=-1))
            parts_max.append(block_max)
            weighted = jnp.einsum(
                "ngc,cd->ngd",
                weights.astype(jnp.bfloat16),
                local_values,
                preferred_element_type=jnp.float32,
            )
            parts_sum.append(weighted.reshape(rows_count, group_width * HEAD_DIMENSION))
        sums_list.append(jnp.concatenate(parts_sum, axis=1))
        maxima_list.append(jnp.concatenate(parts_max, axis=1))
        totals_list.append(jnp.concatenate(parts_total, axis=1))
    new_sums = jnp.stack(sums_list, axis=0)
    new_maxima = jnp.stack(maxima_list, axis=0)
    new_totals = jnp.stack(totals_list, axis=0)
    received = (
        lax.all_to_all(new_sums[None], "blk", split_axis=2, concat_axis=0, tiled=True),
        lax.all_to_all(new_maxima[None], "blk", split_axis=2, concat_axis=0, tiled=True),
        lax.all_to_all(new_totals[None], "blk", split_axis=2, concat_axis=0, tiled=True),
    )
    part_sums, part_max, part_totals = received
    blocks = part_sums.shape[0]
    own_rows = part_sums.shape[2]
    top = jnp.max(part_max, axis=0)
    factor = jnp.exp(part_max - top[None])
    overall = jnp.sum(factor * part_totals, axis=0)
    shaped = part_sums.reshape(blocks, REQUEST_COUNT, own_rows, query_heads, HEAD_DIMENSION)
    merged = jnp.sum(shaped * factor[..., None], axis=0) / overall[..., None]
    own_attention = merged.astype(jnp.bfloat16).reshape(
        REQUEST_COUNT, own_rows, query_heads * HEAD_DIMENSION
    )
    terms = jnp.einsum(
        "rnc,cd->rnd",
        lax.all_gather(own_attention, "blk", axis=1, tiled=True),
        out_weight,
        preferred_element_type=jnp.float32,
    )
    return lax.psum_scatter(terms, "head", scatter_dimension=1, tiled=True).astype(jnp.bfloat16)


def solution(mesh):
    placed = (
        P("groups", "blk", "head"),
        P("groups", "blk", "head"),
        P("groups", "blk", "head"),
        P("head", "blk"),
        P("groups"),
    )
    return jax.shard_map(
        layer, mesh=mesh, in_specs=placed, out_specs=P("groups", "head", "blk"), check_vma=False
    )
```
